32 devices in a mesh: gx: 4 (over x, core), gy: 8 (over z, y).
Axes of the slice: x: 2, y: 2, z: 4, core: 2. Of those that a mesh axis runs over, the one named last changes fastest.
Arguments:
- porous_load_begin: float32 [128, 256, 128], P('gx', 'gy'), may hold values from -6 to 6
- warmth_level_begin: float32 [128, 256, 128], P('gx', 'gy'), may hold values from -6 to 6
- phase_degradation_begin: float32 [128, 256, 128], P('gx', 'gy'), may hold values from 0 to 0.9
- unbroken_conductivity: float32 [128, 256, 128], P('gx', 'gy'), may hold values from 0.1 to 10
- fracture_resistance: float32 [128, 256, 128], P('gx', 'gy'), may hold values from 0.5 to 2
- pumping_inflow_rate: float32 [128, 256, 128], P('gx', 'gy'), may hold values from -18 to 18
- thermal_supply_rate: float32 [128, 256, 128], P('gx', 'gy'), may hold values from -18 to 18
- fracture_zone_patch_roster: int32 [128], P(('gx', 'gy')), may hold values from -1 to 3, as said below
Outputs:
- porous_load_final: float32 [128, 256, 128], P('gx', 'gy')
- warmth_level_final: float32 [128, 256, 128], P('gx', 'gy')
- phase_degradation_final: float32 [128, 256, 128], P('gx', 'gy')
The draws below stay inside these ranges and needn't reach their ends.
Inputs may be any that keep to these rules, and one draw needn't show every extreme that they name: `fracture_zone_patch_roster`: the 4 entries of each device list first distinct local tile indices, then -1 for the rest. Every row of devices along gy lists exactly 16 band tiles in all; in every such row one device lists 4 tiles and one lists none.
All inputs are finite; a program needn't handle non-finite values.
Results may differ from the reference program's by a relative error of at most 0.00002.
Values sent between devices are 32-bit elements; how exact they have to be, the bound alone decides.
A program may use at most 192 MiB of HBM per device.

```python
import math
import jax
import jax.numpy as jnp
from jax import lax

TILE = 32
GRID_EXTENT_Z = 128
SWEEPS = 4
DAMAGE_SWEEPS = 3
CX = 32
CY = 32
TYD = 1
TZD = 4
TPD = 4
GRID_EXTENT_X = 128
GRID_EXTENT_Y = 256
BAND_SLOTS = 128
N_GX = 4
N_GY = 8


def draw_fracture_zone_patch_roster(key, part):
    first, second, third = jax.random.split(key, 3)
    half = TPD // 2
    pair_count = N_GY // 2
    orders = jax.vmap(lambda k: jax.random.permutation(k, N_GY))(jax.random.split(first, N_GX))
    delta = jax.random.randint(second, (N_GX, pair_count), -half, half + 1)
    delta = delta.at[:, 0].set(half)
    rows = jnp.arange(N_GX, dtype=jnp.int32)[:, None]
    counts = jnp.zeros((N_GX, N_GY), jnp.int32)
    counts = counts.at[rows, orders[:, 0::2]].set(half + delta)
    counts = counts.at[rows, orders[:, 1::2]].set(half - delta)
    tiles = jax.vmap(lambda k: jax.random.permutation(k, TPD))(jax.random.split(third, N_GX * N_GY))
    slot = jnp.arange(TPD, dtype=jnp.int32)[None, :]
    listed = jnp.where(slot < counts.reshape(-1)[:, None], tiles, -1)
    return listed.reshape(-1).astype(jnp.int32)


def block_scale(key, extent, cuts, least, largest):
    def one(dim, blocks):
        heights = jax.random.uniform(jax.random.fold_in(jax.random.fold_in(key, 6), dim), (blocks,), jnp.float32, least / len(cuts), largest / len(cuts))
        return jnp.repeat(jnp.exp(heights), extent[dim] // blocks).reshape((-1,) + (1,) * (len(extent) - dim - 1))

    factor_of = one(*cuts[0])
    for cut in cuts[1:]:
        factor_of = factor_of * one(*cut)
    return factor_of


def scatter_about(key, extent, width, bound, cuts=(), kind=jnp.bfloat16):
    values = jax.random.normal(key, extent, jnp.float32) * width
    if len(cuts) > 0:
        values = block_scale(key, extent, cuts, -0.22, 0.18) * values
    return jnp.clip(values, min=-bound, max=bound).astype(kind)


def setup_inputs(seed: int = 0) -> dict:
    key_of = jax.random.split(jax.random.key(seed), 9)
    porous_load_begin = scatter_about(key_of[0], (GRID_EXTENT_X, GRID_EXTENT_Y, GRID_EXTENT_Z), 1.0, 6.0, ((0, 4), (1, 8)), jnp.float32)
    warmth_level_begin = scatter_about(key_of[1], (GRID_EXTENT_X, GRID_EXTENT_Y, GRID_EXTENT_Z), 1.0, 6.0, ((0, 4), (1, 8)), jnp.float32)
    phase_degradation_begin = jnp.clip(0.9 * jax.random.uniform(key_of[2], (GRID_EXTENT_X, GRID_EXTENT_Y, GRID_EXTENT_Z), jnp.float32) ** block_scale(key_of[2], (GRID_EXTENT_X, GRID_EXTENT_Y, GRID_EXTENT_Z), ((0, 4), (1, 8)), -0.2, 0.2), 0.0, 0.9)
    unbroken_conductivity = jnp.clip(jnp.exp(math.log(10.0) - 4.6051702 * jax.random.uniform(key_of[3], (GRID_EXTENT_X, GRID_EXTENT_Y, GRID_EXTENT_Z), jnp.float32) ** block_scale(key_of[3], (GRID_EXTENT_X, GRID_EXTENT_Y, GRID_EXTENT_Z), ((0, 4), (1, 8)), -0.2, 0.2)), 0.1, 10.0)
    fracture_resistance = jnp.clip(jnp.exp(math.log(2.0) - 1.3862944 * jax.random.uniform(key_of[4], (GRID_EXTENT_X, GRID_EXTENT_Y, GRID_EXTENT_Z), jnp.float32) ** block_scale(key_of[4], (GRID_EXTENT_X, GRID_EXTENT_Y, GRID_EXTENT_Z), ((0, 4), (1, 8)), -0.2, 0.2)), 0.5, 2.0)
    pumping_inflow_rate = scatter_about(key_of[5], (GRID_EXTENT_X, GRID_EXTENT_Y, GRID_EXTENT_Z), 3.0, 18.0, ((0, 4), (1, 8)), jnp.float32)
    thermal_supply_rate = scatter_about(key_of[6], (GRID_EXTENT_X, GRID_EXTENT_Y, GRID_EXTENT_Z), 3.0, 18.0, ((0, 4), (1, 8)), jnp.float32)
    fracture_zone_patch_roster = draw_fracture_zone_patch_roster(jax.random.fold_in(key_of[8], 71), 0)
    return {"porous_load_begin": porous_load_begin, "warmth_level_begin": warmth_level_begin, "phase_degradation_begin": phase_degradation_begin, "unbroken_conductivity": unbroken_conductivity, "fracture_resistance": fracture_resistance, "pumping_inflow_rate": pumping_inflow_rate, "thermal_supply_rate": thermal_supply_rate, "fracture_zone_patch_roster": fracture_zone_patch_roster}


liquid_capacity_factor = 0.5
thermal_capacity_factor = 0.5
couple_fluid = 0.3
couple_heat = 0.3
residual_open = 0.05
harmonic_floor = 0.001
crack_length = 2.0
energy_scale = 2.0


def harmonic(left, right):
    return 2.0 * left * right / (left + right + harmonic_floor)


def relax_full(unknown_bundle, conduct, forcing_bundle):
    widths = ((0, 0), (1, 1), (1, 1), (1, 1))
    padded = jnp.pad(unknown_bundle, widths)
    conduct_pad = jnp.pad(conduct, widths)
    pairs = [
        (conduct_pad[:, 2:, 1:-1, 1:-1], padded[:, 2:, 1:-1, 1:-1]),
        (conduct_pad[:, :-2, 1:-1, 1:-1], padded[:, :-2, 1:-1, 1:-1]),
        (conduct_pad[:, 1:-1, 2:, 1:-1], padded[:, 1:-1, 2:, 1:-1]),
        (conduct_pad[:, 1:-1, :-2, 1:-1], padded[:, 1:-1, :-2, 1:-1]),
        (conduct_pad[:, 1:-1, 1:-1, 2:], padded[:, 1:-1, 1:-1, 2:]),
        (conduct_pad[:, 1:-1, 1:-1, :-2], padded[:, 1:-1, 1:-1, :-2]),
    ]
    flux = jnp.zeros_like(unknown_bundle)
    weight_sum = jnp.zeros_like(unknown_bundle)
    for other, value in pairs:
        weight = harmonic(conduct, other)
        flux = flux + weight * value
        weight_sum = weight_sum + weight
    coupling = jnp.stack([couple_fluid * unknown_bundle[1], couple_heat * unknown_bundle[0]])
    storage = jnp.array([liquid_capacity_factor, thermal_capacity_factor], jnp.float32)[:, None, None, None]
    return (forcing_bundle + flux + coupling) / (storage + weight_sum)


def tile_sweeps(block):
    values = block[0]
    drive = block[1, 1:-1, 1:-1, 1:-1]
    tough = block[2, 1:-1, 1:-1, 1:-1]
    spread = tough * crack_length
    denom = tough / crack_length + drive + 6.0 * spread
    inner = values[1:-1, 1:-1, 1:-1]
    for step in range(DAMAGE_SWEEPS):
        near = values[2:, 1:-1, 1:-1] + values[:-2, 1:-1, 1:-1]
        near = near + values[1:-1, 2:, 1:-1] + values[1:-1, :-2, 1:-1]
        near = near + values[1:-1, 1:-1, 2:] + values[1:-1, 1:-1, :-2]
        inner = (drive + spread * near) / denom
        values = values.at[1:-1, 1:-1, 1:-1].set(inner)
    return inner


def reference(porous_load_begin, warmth_level_begin, phase_degradation_begin, unbroken_conductivity, fracture_resistance, pumping_inflow_rate, thermal_supply_rate, fracture_zone_patch_roster):
    openness = (1.0 - phase_degradation_begin) ** 2 + residual_open
    mobility = unbroken_conductivity * openness
    conduct = jnp.stack([mobility, openness])
    forcing_bundle = jnp.stack([pumping_inflow_rate + liquid_capacity_factor * porous_load_begin, thermal_supply_rate + thermal_capacity_factor * warmth_level_begin])
    unknown_bundle = jnp.stack([porous_load_begin, warmth_level_begin])
    for step in range(SWEEPS):
        unknown_bundle = relax_full(unknown_bundle, conduct, forcing_bundle)
    porous_load_final = unknown_bundle[0]
    warmth_level_final = unknown_bundle[1]
    drive = 2.0 * energy_scale * porous_load_final * porous_load_final
    fields = jnp.stack([jnp.pad(phase_degradation_begin, 1), jnp.pad(drive, 1), jnp.pad(fracture_resistance, 1)])
    zero = jnp.zeros((), jnp.int32)

    def update(index, phase_degradation_final):
        index = jnp.asarray(index).astype(jnp.int32)
        local = fracture_zone_patch_roster[index].astype(jnp.int32)
        valid = local >= 0
        tile = jnp.maximum(local, 0)
        device = index // TPD
        row_x = device // N_GY
        row_y = device % N_GY
        tile_a = tile // (TYD * TZD)
        tile_b = (tile // TZD) % TYD
        tile_c = tile % TZD
        start_x = (row_x * CX + tile_a * TILE).astype(jnp.int32)
        start_y = (row_y * CY + tile_b * TILE).astype(jnp.int32)
        start_z = (tile_c * TILE).astype(jnp.int32)
        block = lax.dynamic_slice(fields, (zero, start_x, start_y, start_z), (3, TILE + 2, TILE + 2, TILE + 2))
        inner = tile_sweeps(block)
        before = lax.dynamic_slice(phase_degradation_final, (start_x, start_y, start_z), (TILE, TILE, TILE))
        return lax.dynamic_update_slice(phase_degradation_final, jnp.where(valid, inner, before), (start_x, start_y, start_z))

    phase_degradation_final = lax.fori_loop(0, BAND_SLOTS, update, phase_degradation_begin)
    return porous_load_final, warmth_level_final, phase_degradation_final
```

```python
import functools

import jax
import jax.numpy as jnp
from jax import lax
from jax.experimental import pallas as pl
from jax.experimental.pallas import tpu as pltpu
from jax.sharding import PartitionSpec as P

TILE = 32
SWEEPS = 4
DAMAGE_SWEEPS = 3
CHUNKS = 4

capacity = (0.5, 0.5)
couple = (0.3, 0.3)
residual_open = 0.05
harmonic_floor = 0.001
crack_length = 2.0
energy_scale = 2.0
F32 = jnp.float32


def harmonic(left, right):
    return 2.0 * left * right / (left + right + harmonic_floor)


def kernel(
    names,
    sizes,
    p_hbm,
    t_hbm,
    d_hbm,
    k_hbm,
    g_hbm,
    qp_hbm,
    qt_hbm,
    roster_hbm,
    final,
    damage,
    around,
    tough,
    listed,
    state,
    fixed,
    force,
    conduct,
    wx,
    wy,
    wz,
    den,
    inv,
    hwx,
    hwy,
    ysend0,
    yrecv0,
    xrecv0,
    ysend,
    yrecv,
    xrecv,
    roster,
    in_sem,
    xs0,
    xr0,
    ys0,
    yr0,
    xs,
    xr,
    ys,
    yr,
):
    nx, ny, nz, count_x, count_y = sizes
    cells = nx * ny
    gx, gy = names
    ix = lax.axis_index(gx)
    iy = lax.axis_index(gy)
    has_x = (ix > 0, ix < count_x - 1)
    has_y = (iy > 0, iy < count_y - 1)
    to_x = ({gx: ix - 1}, {gx: ix + 1})
    to_y = ({gy: iy - 1}, {gy: iy + 1})
    mesh_type = pl.DeviceIdType.MESH

    loads = [
        pltpu.make_async_copy(d_hbm, damage.at[pl.ds(ny, cells)], in_sem.at[0]),
        pltpu.make_async_copy(k_hbm, fixed.at[0], in_sem.at[1]),
        pltpu.make_async_copy(p_hbm, state.at[0, 0], in_sem.at[2]),
        pltpu.make_async_copy(t_hbm, state.at[0, 1], in_sem.at[3]),
        pltpu.make_async_copy(qp_hbm, fixed.at[1], in_sem.at[4]),
        pltpu.make_async_copy(qt_hbm, fixed.at[2], in_sem.at[5]),
        pltpu.make_async_copy(g_hbm, tough, in_sem.at[6]),
        pltpu.make_async_copy(roster_hbm, roster, in_sem.at[7]),
    ]
    for load in loads[:4]:
        load.start()

    barrier = pltpu.get_barrier_semaphore()
    for has, to in ((has_x, to_x), (has_y, to_y)):
        for side in range(2):

            @pl.when(has[side])
            def _():
                pl.semaphore_signal(barrier, inc=1, device_id=to[side], device_id_type=mesh_type)

    for side in range(2):

        @pl.when(jnp.logical_not(has_x[side]))
        def _():
            xrecv0[side] = jnp.zeros(xrecv0.shape[1:], F32)
            for step in range(SWEEPS - 1):
                xrecv[step, side] = jnp.zeros(xrecv.shape[2:], F32)

        @pl.when(jnp.logical_not(has_y[side]))
        def _():
            yrecv0[side] = jnp.zeros(yrecv0.shape[1:], F32)
            for step in range(SWEEPS - 1):
                yrecv[step, side] = jnp.zeros(yrecv.shape[2:], F32)

    zero_plane = jnp.zeros((ny, nz), F32)
    damage[0:ny] = zero_plane
    damage[(nx + 1) * ny : (nx + 2) * ny] = zero_plane
    for f in range(2):
        wx[f, 0:ny] = zero_plane
        wx[f, nx * ny : (nx + 1) * ny] = zero_plane

    edge_row = (pl.ds(0, nx, stride=ny), pl.ds(ny - 1, nx, stride=ny))
    edge_pad = (pl.ds(ny, nx, stride=ny), pl.ds(2 * ny - 1, nx, stride=ny))
    edge_plane = (pl.ds(0, ny), pl.ds((nx - 1) * ny, ny))
    edge_plane_pad = (pl.ds(ny, ny), pl.ds(nx * ny, ny))

    for load in loads[:4]:
        load.wait()
    for load in loads[4:]:
        load.start()

    for side in range(2):
        ysend0[side, 0 * nx : 1 * nx] = damage[edge_pad[side], :]
        ysend0[side, 1 * nx : 2 * nx] = fixed.at[0][edge_row[side], :]
        ysend0[side, 2 * nx : 3 * nx] = state.at[0, 0][edge_row[side], :]
        ysend0[side, 3 * nx : 4 * nx] = state.at[0, 1][edge_row[side], :]

    peers = sum(jnp.where(has, 1, 0).astype(jnp.int32) for has in has_x + has_y)
    pl.semaphore_wait(barrier, peers)

    parts0 = ((0, 2 * nx), (2 * nx, nx), (3 * nx, nx))

    def y_copy0(side, slot):
        return [
            pltpu.make_async_remote_copy(
                src_ref=ysend0.at[side, pl.ds(start, size)],
                dst_ref=yrecv0.at[slot, pl.ds(start, size)],
                send_sem=ys0.at[side, n],
                recv_sem=yr0.at[slot, n],
                device_id=to_y[side],
                device_id_type=mesh_type,
            )
            for n, (start, size) in enumerate(parts0)
        ]

    def x_copy0(side, slot):
        sources = (
            damage.at[edge_plane_pad[side]],
            fixed.at[0, edge_plane[side]],
            state.at[0, 0, edge_plane[side]],
            state.at[0, 1, edge_plane[side]],
        )
        return [
            pltpu.make_async_remote_copy(
                src_ref=source,
                dst_ref=xrecv0.at[slot, pl.ds(n * ny, ny)],
                send_sem=xs0.at[side, n],
                recv_sem=xr0.at[slot, n],
                device_id=to_x[side],
                device_id_type=mesh_type,
            )
            for n, source in enumerate(sources)
        ]

    def y_copy(step, f, side, slot):
        return pltpu.make_async_remote_copy(
            src_ref=ysend.at[step, side, pl.ds(f * nx, nx)],
            dst_ref=yrecv.at[step, slot, pl.ds(f * nx, nx)],
            send_sem=ys.at[step, side, f],
            recv_sem=yr.at[step, slot, f],
            device_id=to_y[side],
            device_id_type=mesh_type,
        )

    def x_copy(step, side, slot):
        return [
            pltpu.make_async_remote_copy(
                src_ref=state.at[step + 1, f, edge_plane[side]],
                dst_ref=xrecv.at[step, slot, pl.ds(f * ny, ny)],
                send_sem=xs.at[step, side, f],
                recv_sem=xr.at[step, slot, f],
                device_id=to_x[side],
                device_id_type=mesh_type,
            )
            for f in range(2)
        ]

    for side in range(2):

        @pl.when(has_y[side])
        def _():
            for copy in y_copy0(side, 1 - side):
                copy.start()

    for side in range(2):

        @pl.when(has_x[side])
        def _():
            for copy in x_copy0(side, 1 - side):
                copy.start()

    row = lax.broadcasted_iota(jnp.int32, (ny, nz), 0)
    lane = lax.broadcasted_iota(jnp.int32, (ny, nz), 1)

    def at(i):
        return pl.ds(pl.multiple_of(i * ny, ny), ny)

    def open_of(d):
        return (1.0 - d) * (1.0 - d) + residual_open

    for load in loads[4:6]:
        load.wait()

    @pl.loop(0, nx, unroll=8)
    def _(i):
        openness = open_of(damage[at(i + 1)])
        conduct[1, at(i)] = openness
        conduct[0, at(i)] = fixed[0, at(i)] * openness
        for f in range(2):
            force[f, at(i)] = fixed[1 + f, at(i)] + capacity[f] * state[0, f, at(i)]

    @pl.loop(0, nx, unroll=8)
    def _(i):
        follow = jnp.minimum(i + 1, nx - 1)
        inside = jnp.where(i < nx - 1, 1.0, 0.0).astype(F32)
        for f in range(2):
            own = conduct[f, at(i)]
            ahead = harmonic(own, conduct[f, at(follow)]) * inside
            wx[f, at(i + 1)] = ahead
            y_hi = jnp.where(row < ny - 1, harmonic(own, pltpu.roll(own, ny - 1, 0)), 0.0)
            y_lo = pltpu.roll(y_hi, 1, 0)
            z_hi = jnp.where(lane < nz - 1, harmonic(own, pltpu.roll(own, nz - 1, 1)), 0.0)
            z_lo = pltpu.roll(z_hi, 1, 1)
            wy[f, 0, at(i)] = y_lo
            wy[f, 1, at(i)] = y_hi
            wz[f, 0, at(i)] = z_lo
            wz[f, 1, at(i)] = z_hi
            total = capacity[f] + ahead + wx[f, at(i)] + y_lo + y_hi + z_lo + z_hi
            den[f, at(i)] = total
            inv[f, at(i)] = 1.0 / total

    levels = [state.at[step] for step in range(SWEEPS)] + [final]

    def sweep(step):
        @pl.loop(0, nx, unroll=8)
        def _(i):
            before = jnp.maximum(i - 1, 0)
            follow = jnp.minimum(i + 1, nx - 1)
            center = [state[step, f, at(i)] for f in range(2)]
            for f in range(2):
                c = center[f]
                acc = force[f, at(i)] + couple[f] * center[1 - f]
                acc = acc + wx[f, at(i)] * state[step, f, at(before)]
                acc = acc + wx[f, at(i + 1)] * state[step, f, at(follow)]
                acc = acc + wy[f, 0, at(i)] * pltpu.roll(c, 1, 0)
                acc = acc + wy[f, 1, at(i)] * pltpu.roll(c, ny - 1, 0)
                acc = acc + wz[f, 0, at(i)] * pltpu.roll(c, 1, 1)
                acc = acc + wz[f, 1, at(i)] * pltpu.roll(c, nz - 1, 1)
                levels[step + 1][f, at(i)] = acc * inv[f, at(i)]

    def send_y(step, f, side):
        @pl.when(has_y[side])
        def _():
            y_copy(step, f, side, 1 - side).start()

    def send_x(step, f):
        for side in range(2):

            @pl.when(has_x[side])
            def _():
                x_copy(step, side, 1 - side)[f].start()

    sweep(0)
    for side in range(2):

        @pl.when(has_x[side])
        def _():
            for copy in x_copy0(side, side):
                copy.wait_recv()

    for side in range(2):
        there = jnp.where(has_x[side], 1.0, 0.0).astype(F32)
        openness = open_of(xrecv0[side, 0:ny]) * there
        halo_conduct = (xrecv0[side, ny : 2 * ny] * openness, openness)
        cut = edge_plane[side]
        for f in range(2):
            w = harmonic(conduct[f, cut], halo_conduct[f])
            hwx[f, side] = w
            old = den[f, cut]
            total = old + w
            inverse = 1.0 / total
            den[f, cut] = total
            inv[f, cut] = inverse
            value = xrecv0[side, (2 + f) * ny : (3 + f) * ny]
            state[1, f, cut] = (state[1, f, cut] * old + w * value) * inverse

    for side in range(2):

        @pl.when(has_y[side])
        def _():
            y_copy0(side, side)[0].wait_recv()

    halo_conduct = []
    for side in range(2):
        there = jnp.where(has_y[side], 1.0, 0.0).astype(F32)
        openness = open_of(yrecv0[side, 0:nx]) * there
        halo_conduct.append((yrecv0[side, nx : 2 * nx] * openness, openness))
    for f in range(2):
        for side in range(2):
            cut = edge_row[side]
            w = harmonic(conduct.at[f][cut, :], halo_conduct[side][f])
            hwy[f, side] = w
            old = den.at[f][cut, :]
            total = old + w
            inverse = 1.0 / total
            inv.at[f][cut, :] = inverse

            @pl.when(has_y[side])
            def _():
                y_copy0(side, side)[1 + f].wait_recv()

            value = yrecv0[side, (2 + f) * nx : (3 + f) * nx]
            fresh = (state.at[1, f][cut, :] * old + w * value) * inverse
            state.at[1, f][cut, :] = fresh
            ysend[0, side, f * nx : (f + 1) * nx] = fresh
            send_y(0, f, side)
        send_x(0, f)

    for step in range(1, SWEEPS):
        sweep(step)
        if step == 1:
            at_low = lane % TILE == 0
            at_high = lane % TILE == TILE - 1

            @pl.loop(0, nx, unroll=8)
            def _(i):
                d = damage[at(i + 1)]
                low = jnp.where(at_low & (lane > 0), pltpu.roll(d, 1, 1), 0.0)
                high = jnp.where(at_high & (lane < nz - 1), pltpu.roll(d, nz - 1, 1), 0.0)
                around[at(i)] = low + high

            for side in range(2):
                around[edge_plane[side], :] = around[edge_plane[side], :] + xrecv0[side, 0:ny]
            for side in range(2):
                around[edge_row[side], :] = around[edge_row[side], :] + yrecv0[side, 0:nx]
            loads[6].wait()
            loads[7].wait()
            tile_of = lane // TILE
            chosen = tile_of == roster[0]
            for n in range(1, roster.shape[0]):
                chosen = chosen | (tile_of == roster[n])
            listed[...] = jnp.where(chosen, 1.0, 0.0)
        for side in range(2):

            @pl.when(has_x[side])
            def _():
                for copy in x_copy(step - 1, side, side):
                    copy.wait_recv()

        for side in range(2):
            cut = edge_plane[side]
            for f in range(2):
                value = xrecv[step - 1, side, f * ny : (f + 1) * ny]
                levels[step + 1][f, cut] = (
                    levels[step + 1][f, cut] + hwx[f, side] * value * inv[f, cut]
                )

        for f in range(2):
            for side in range(2):
                cut = edge_row[side]
                scale = hwy[f, side] * inv.at[f][cut, :]

                @pl.when(has_y[side])
                def _():
                    y_copy(step - 1, f, side, side).wait_recv()

                value = yrecv[step - 1, side, f * nx : (f + 1) * nx]
                fresh = levels[step + 1].at[f][cut, :] + scale * value
                levels[step + 1].at[f][cut, :] = fresh
                if step < SWEEPS - 1:
                    ysend[step, side, f * nx : (f + 1) * nx] = fresh
                    send_y(step, f, side)
            if step < SWEEPS - 1:
                send_x(step, f)

    for side in range(2):

        @pl.when(has_y[side])
        def _():
            for copy in y_copy0(side, 1 - side):
                copy.wait_send()
            for step in range(SWEEPS - 1):
                for f in range(2):
                    y_copy(step, f, side, 1 - side).wait_send()

        @pl.when(has_x[side])
        def _():
            for copy in x_copy0(side, 1 - side):
                copy.wait_send()
            for step in range(SWEEPS - 1):
                for copy in x_copy(step, side, 1 - side):
                    copy.wait_send()


def finish(
    sizes,
    final,
    damage,
    around,
    tough,
    listed,
    p_out,
    t_out,
    d_out,
    work,
    da,
    db,
    out_sem,
):
    nx, ny, nz = sizes
    cells = nx * ny
    row = lax.broadcasted_iota(jnp.int32, (ny, nz), 0)
    lane = lax.broadcasted_iota(jnp.int32, (ny, nz), 1)

    def at(i):
        return pl.ds(pl.multiple_of(i * ny, ny), ny)

    outs = [
        pltpu.make_async_copy(final.at[0], p_out, out_sem.at[0]),
        pltpu.make_async_copy(final.at[1], t_out, out_sem.at[1]),
    ]
    for out in outs:
        out.start()

    zero_plane = jnp.zeros((ny, nz), F32)
    for which in range(2):
        work[which, 0:ny] = zero_plane
        work[which, (nx + 1) * ny : (nx + 2) * ny] = zero_plane

    y_first = row == 0
    y_last = row == ny - 1
    z_first = lane % TILE == 0
    z_last = lane % TILE == TILE - 1
    inside = listed[...] > 0.0

    piece = cells // CHUNKS
    last = [
        pltpu.make_async_copy(
            work.at[0, pl.ds(ny + chunk * piece, piece)],
            d_out.at[pl.ds(chunk * piece, piece)],
            out_sem.at[2 + chunk],
        )
        for chunk in range(CHUNKS)
    ]
    for step in range(DAMAGE_SWEEPS):
        source = (damage, work.at[0], work.at[1])[step % 3]
        target = (work.at[0], work.at[1], work.at[0])[step % 3]

        def relax(i):
            d = source[at(i + 1)]
            near = around[at(i)] + source[at(i)] + source[at(i + 2)]
            near = near + jnp.where(y_first, 0.0, pltpu.roll(d, 1, 0))
            near = near + jnp.where(y_last, 0.0, pltpu.roll(d, ny - 1, 0))
            near = near + jnp.where(z_first, 0.0, pltpu.roll(d, 1, 1))
            near = near + jnp.where(z_last, 0.0, pltpu.roll(d, nz - 1, 1))
            if step == 0:
                load = final[0, at(i)]
                hard = tough[at(i)]
                drive = 2.0 * energy_scale * load * load
                spread = hard * crack_length
                inverse = 1.0 / (hard / crack_length + drive + 6.0 * spread)
                a = drive * inverse
                b = spread * inverse
                da[at(i)] = a
                db[at(i)] = b
            else:
                a = da[at(i)]
                b = db[at(i)]
            fresh = a + b * near
            if step == DAMAGE_SWEEPS - 1:
                fresh = jnp.where(inside, fresh, damage[at(i + 1)])
            target[at(i + 1)] = fresh

        if step < DAMAGE_SWEEPS - 1:
            pl.loop(0, nx, unroll=8)(relax)
        else:
            for chunk in range(CHUNKS):
                pl.loop(chunk * nx // CHUNKS, (chunk + 1) * nx // CHUNKS, unroll=8)(relax)
                last[chunk].start()

    for out in outs:
        out.wait()
    for out in last:
        out.wait()


def body(counts, names, *arrays):
    nx, ny, nz = arrays[0].shape
    cells = nx * ny
    flat = [a.reshape(cells, nz) for a in arrays[:-1]] + [arrays[-1]]
    flat = [pltpu.with_memory_space_constraint(a, pltpu.HBM) for a in flat]
    block = jax.ShapeDtypeStruct((cells, nz), F32)
    dma = pltpu.SemaphoreType.DMA
    steps = SWEEPS - 1
    vmem = pl.BlockSpec(memory_space=pltpu.VMEM)
    hbm = pl.BlockSpec(memory_space=pl.ANY)
    middle = pl.pallas_call(
        functools.partial(kernel, names, (nx, ny, nz) + counts),
        out_shape=(
            jax.ShapeDtypeStruct((2, cells, nz), F32),
            jax.ShapeDtypeStruct((cells + 2 * ny, nz), F32),
            block,
            block,
            jax.ShapeDtypeStruct((ny, nz), F32),
        ),
        in_specs=[hbm] * 8,
        out_specs=[vmem] * 5,
        scratch_shapes=[
            pltpu.VMEM((SWEEPS, 2, cells, nz), F32),
            pltpu.VMEM((3, cells, nz), F32),
            pltpu.VMEM((2, cells, nz), F32),
            pltpu.VMEM((2, cells, nz), F32),
            pltpu.VMEM((2, cells + ny, nz), F32),
            pltpu.VMEM((2, 2, cells, nz), F32),
            pltpu.VMEM((2, 2, cells, nz), F32),
            pltpu.VMEM((2, cells, nz), F32),
            pltpu.VMEM((2, cells, nz), F32),
            pltpu.VMEM((2, 2, ny, nz), F32),
            pltpu.VMEM((2, 2, nx, nz), F32),
            pltpu.VMEM((2, 4 * nx, nz), F32),
            pltpu.VMEM((2, 4 * nx, nz), F32),
            pltpu.VMEM((2, 4 * ny, nz), F32),
            pltpu.VMEM((steps, 2, 2 * nx, nz), F32),
            pltpu.VMEM((steps, 2, 2 * nx, nz), F32),
            pltpu.VMEM((steps, 2, 2 * ny, nz), F32),
            pltpu.SMEM(arrays[-1].shape, jnp.int32),
            dma((8,)),
            dma((2, 4)),
            dma((2, 4)),
            dma((2, 3)),
            dma((2, 3)),
            dma((steps, 2, 2)),
            dma((steps, 2, 2)),
            dma((steps, 2, 2)),
            dma((steps, 2, 2)),
        ],
        compiler_params=pltpu.CompilerParams(
            collective_id=0, has_side_effects=True, vmem_limit_bytes=40 * 2**20
        ),
    )(*flat)
    outs = pl.pallas_call(
        functools.partial(finish, (nx, ny, nz)),
        out_shape=(block, block, block),
        in_specs=[vmem] * 5,
        out_specs=[hbm] * 3,
        scratch_shapes=[
            pltpu.VMEM((2, cells + 2 * ny, nz), F32),
            pltpu.VMEM((cells, nz), F32),
            pltpu.VMEM((cells, nz), F32),
            dma((2 + CHUNKS,)),
        ],
        compiler_params=pltpu.CompilerParams(vmem_limit_bytes=16 * 2**20),
    )(*middle)
    return tuple(o.reshape(nx, ny, nz) for o in outs)


def solution(mesh):
    cut = P("gx", "gy", None)
    names = ("gx", "gy")
    counts = (mesh.shape["gx"], mesh.shape["gy"])
    return jax.shard_map(
        functools.partial(body, counts, names),
        mesh=mesh,
        in_specs=(cut,) * 7 + (P(("gx", "gy")),),
        out_specs=(cut, cut, cut),
        check_vma=False,
    )
```

```python
import functools

import jax
import jax.numpy as jnp
from jax import lax
from jax.experimental import pallas as pl
from jax.experimental.pallas import tpu as pltpu
from jax.sharding import PartitionSpec as P

TILE = 32
SWEEPS = 4
DAMAGE_SWEEPS = 3
CHUNKS = 4
ONE, TWO, PART, INV = range(4)
SENDS = 4

capacity = (0.5, 0.5)
couple = (0.3, 0.3)
residual_open = 0.05
harmonic_floor = 0.001
crack_length = 2.0
energy_scale = 2.0
F32 = jnp.float32


def harmonic(left, right):
    return 2.0 * left * right / (left + right + harmonic_floor)


def kernel(
    names,
    sizes,
    p_hbm,
    t_hbm,
    d_hbm,
    k_hbm,
    g_hbm,
    qp_hbm,
    qt_hbm,
    roster_hbm,
    final,
    damage,
    around,
    tough,
    listed,
    state,
    fixed,
    force,
    conduct,
    wx,
    wy,
    wz,
    den,
    inv,
    hwx,
    hwy,
    xface,
    yface,
    ysend0,
    yrecv0,
    xrecv0,
    ysend,
    yrecv,
    xsend,
    xrecv,
    csend,
    crecv,
    roster,
    in_sem,
    send_sem,
    xr,
    yr,
    cr,
):
    nx, ny, nz, count_x, count_y = sizes
    cells = nx * ny
    gx, gy = names
    ix = lax.axis_index(gx)
    iy = lax.axis_index(gy)
    has_x = (ix > 0, ix < count_x - 1)
    has_y = (iy > 0, iy < count_y - 1)
    to_x = ({gx: ix - 1}, {gx: ix + 1})
    to_y = ({gy: iy - 1}, {gy: iy + 1})
    corners = [(sx, sy) for sx in range(2) for sy in range(2)]
    has_c = [has_x[sx] & has_y[sy] for sx, sy in corners]
    to_c = [to_x[sx] | to_y[sy] for sx, sy in corners]
    mesh_type = pl.DeviceIdType.MESH

    barrier = pltpu.get_barrier_semaphore()
    for has, to in ((has_y, to_y), (has_x, to_x)):
        for side in range(2):

            @pl.when(has[side])
            def _():
                pl.semaphore_signal(barrier, inc=1, device_id=to[side], device_id_type=mesh_type)

    load = pltpu.make_async_copy
    first = [
        load(d_hbm, damage.at[pl.ds(ny, cells)], in_sem.at[0]),
        load(k_hbm, fixed.at[0], in_sem.at[0]),
        load(p_hbm, state.at[0, 0], in_sem.at[0]),
        load(t_hbm, state.at[0, 1], in_sem.at[0]),
    ]
    rates = [
        load(qp_hbm, fixed.at[1], in_sem.at[1]),
        load(qt_hbm, fixed.at[2], in_sem.at[1]),
    ]
    late = [
        load(g_hbm, tough, in_sem.at[2]),
        load(roster_hbm, roster, in_sem.at[3]),
    ]
    for copy in first:
        copy.start()

    def arrived(ref, sem):
        pltpu.make_async_copy(ref, ref, sem).wait()

    csend[...] = jnp.zeros(csend.shape, F32)
    for c in range(4):

        @pl.when(jnp.logical_not(has_c[c]))
        def _():
            crecv[c] = jnp.zeros(crecv.shape[1:], F32)

    for side in range(2):

        @pl.when(jnp.logical_not(has_x[side]))
        def _():
            xrecv0[side] = jnp.zeros(xrecv0.shape[1:], F32)
            for step in range(SENDS):
                xrecv[side, step] = jnp.zeros(xrecv.shape[2:], F32)

        @pl.when(jnp.logical_not(has_y[side]))
        def _():
            yrecv0[side] = jnp.zeros(yrecv0.shape[1:], F32)
            for step in range(SENDS):
                yrecv[side, step] = jnp.zeros(yrecv.shape[2:], F32)

    zero_plane = jnp.zeros((ny, nz), F32)
    damage[0:ny] = zero_plane
    damage[(nx + 1) * ny : (nx + 2) * ny] = zero_plane
    for f in range(2):
        wx[f, 0:ny] = zero_plane
        wx[f, nx * ny : (nx + 1) * ny] = zero_plane

    def rows(r, first_plane=0):
        return pl.ds(first_plane * ny + r, nx, stride=ny)

    def plane(i):
        return pl.ds(i * ny, ny)

    edge_row = (rows(0), rows(ny - 1))
    next_row = (rows(1), rows(ny - 2))
    edge_plane = (plane(0), plane(nx - 1))
    next_plane = (plane(1), plane(nx - 2))
    edge_pad = (rows(0, 1), rows(ny - 1, 1))
    edge_plane_pad = (plane(1), plane(nx))

    arrived(state.at[pl.ds(0, 2)], in_sem.at[0])
    for copy in rates + late:
        copy.start()

    for side in range(2):
        ysend0[side, 0 * nx : 1 * nx] = damage[edge_pad[side], :]
        ysend0[side, 1 * nx : 2 * nx] = fixed.at[0][edge_row[side], :]
        ysend0[side, 2 * nx : 3 * nx] = state.at[0, 0][edge_row[side], :]
        ysend0[side, 3 * nx : 4 * nx] = state.at[0, 1][edge_row[side], :]

    def remote(source, target, send, recv, to):
        return pltpu.make_async_remote_copy(
            src_ref=source,
            dst_ref=target,
            send_sem=send,
            recv_sem=recv,
            device_id=to,
            device_id_type=mesh_type,
        )

    place = {ONE: 2, TWO: 3, PART: 4, INV: 4}

    def send_y(step, side):
        @pl.when(has_y[side])
        def _():
            remote(
                ysend.at[side, step],
                yrecv.at[1 - side, step],
                send_sem.at[2 + side],
                yr.at[1 - side, place[step]],
                to_y[side],
            ).start()

    def send_x(step, side, sources):
        @pl.when(has_x[side])
        def _():
            for f in range(2):
                remote(
                    sources[f],
                    xrecv.at[1 - side, step, pl.ds(f * ny, ny)],
                    send_sem.at[side],
                    xr.at[1 - side, place[step] - 1],
                    to_x[side],
                ).start()

    def wait_y(side, ref, n):
        @pl.when(has_y[side])
        def _():
            arrived(ref, yr.at[side, n])

    def wait_x(side, ref, n):
        @pl.when(has_x[side])
        def _():
            arrived(ref, xr.at[side, n])

    peers = sum(jnp.where(has, 1, 0).astype(jnp.int32) for has in has_x + has_y)
    pl.semaphore_wait(barrier, peers)

    for half in range(2):
        for side in range(2):

            @pl.when(has_y[side])
            def _():
                part = pl.ds(half * 2 * nx, 2 * nx)
                remote(
                    ysend0.at[side, part],
                    yrecv0.at[1 - side, part],
                    send_sem.at[2 + side],
                    yr.at[1 - side, half],
                    to_y[side],
                ).start()

    for side in range(2):
        sources = (
            damage.at[edge_plane_pad[side]],
            fixed.at[0, edge_plane[side]],
            state.at[0, 0, edge_plane[side]],
            state.at[0, 1, edge_plane[side]],
        )

        @pl.when(has_x[side])
        def _():
            for n, source in enumerate(sources):
                remote(
                    source,
                    xrecv0.at[1 - side, pl.ds(n * ny, ny)],
                    send_sem.at[side],
                    xr.at[1 - side, 0],
                    to_x[side],
                ).start()

    row = lax.broadcasted_iota(jnp.int32, (ny, nz), 0)
    lane = lax.broadcasted_iota(jnp.int32, (ny, nz), 1)

    def at(i):
        return pl.ds(pl.multiple_of(i * ny, ny), ny)

    def open_of(d):
        return (1.0 - d) * (1.0 - d) + residual_open

    arrived(fixed.at[pl.ds(1, 2)], in_sem.at[1])

    @pl.loop(0, nx, unroll=8)
    def _(i):
        openness = open_of(damage[at(i + 1)])
        conduct[1, at(i)] = openness
        conduct[0, at(i)] = fixed[0, at(i)] * openness
        for f in range(2):
            force[f, at(i)] = fixed[1 + f, at(i)] + capacity[f] * state[0, f, at(i)]

    @pl.loop(0, nx, unroll=8)
    def _(i):
        follow = jnp.minimum(i + 1, nx - 1)
        inside = jnp.where(i < nx - 1, 1.0, 0.0).astype(F32)
        for f in range(2):
            own = conduct[f, at(i)]
            ahead = harmonic(own, conduct[f, at(follow)]) * inside
            wx[f, at(i + 1)] = ahead
            y_hi = jnp.where(row < ny - 1, harmonic(own, pltpu.roll(own, ny - 1, 0)), 0.0)
            y_lo = pltpu.roll(y_hi, 1, 0)
            z_hi = jnp.where(lane < nz - 1, harmonic(own, pltpu.roll(own, nz - 1, 1)), 0.0)
            z_lo = pltpu.roll(z_hi, 1, 1)
            wy[f, 0, at(i)] = y_lo
            wy[f, 1, at(i)] = y_hi
            wz[f, 0, at(i)] = z_lo
            wz[f, 1, at(i)] = z_hi
            total = capacity[f] + ahead + wx[f, at(i)] + y_lo + y_hi + z_lo + z_hi
            den[f, at(i)] = total
            inv[f, at(i)] = 1.0 / total

    levels = [state.at[step] for step in range(SWEEPS)] + [final]

    def sweep(step):
        @pl.loop(0, nx, unroll=8)
        def _(i):
            before = jnp.maximum(i - 1, 0)
            follow = jnp.minimum(i + 1, nx - 1)
            center = [state[step, f, at(i)] for f in range(2)]
            for f in range(2):
                c = center[f]
                acc = force[f, at(i)] + couple[f] * center[1 - f]
                acc = acc + wx[f, at(i)] * state[step, f, at(before)]
                acc = acc + wx[f, at(i + 1)] * state[step, f, at(follow)]
                acc = acc + wy[f, 0, at(i)] * pltpu.roll(c, 1, 0)
                acc = acc + wy[f, 1, at(i)] * pltpu.roll(c, ny - 1, 0)
                acc = acc + wz[f, 0, at(i)] * pltpu.roll(c, 1, 1)
                acc = acc + wz[f, 1, at(i)] * pltpu.roll(c, nz - 1, 1)
                levels[step + 1][f, at(i)] = acc * inv[f, at(i)]

    sweep(0)
    for side in range(2):
        wait_x(side, xrecv0.at[side], 0)

    for side in range(2):
        there = jnp.where(has_x[side], 1.0, 0.0).astype(F32)
        openness = open_of(xrecv0[side, 0:ny]) * there
        halo_conduct = (xrecv0[side, ny : 2 * ny] * openness, openness)
        cut = edge_plane[side]
        for f in range(2):
            w = harmonic(conduct[f, cut], halo_conduct[f])
            hwx[f, side] = w
            old = den[f, cut]
            total = old + w
            inverse = 1.0 / total
            den[f, cut] = total
            inv[f, cut] = inverse
            value = xrecv0[side, (2 + f) * ny : (3 + f) * ny]
            state[1, f, cut] = (state[1, f, cut] * old + w * value) * inverse

    for side in range(2):
        wait_y(side, yrecv0.at[side, pl.ds(0, 2 * nx)], 0)

    fresh_parts = []
    for side in range(2):
        there = jnp.where(has_y[side], 1.0, 0.0).astype(F32)
        openness = open_of(yrecv0[side, 0:nx]) * there
        halo_conduct = (yrecv0[side, nx : 2 * nx] * openness, openness)
        cut = edge_row[side]
        for f in range(2):
            w = harmonic(conduct.at[f][cut, :], halo_conduct[f])
            hwy[f, side] = w
            old = den.at[f][cut, :]
            inverse = 1.0 / (old + w)
            inv.at[f][cut, :] = inverse
            fresh_parts.append((state.at[1, f][cut, :] * old * inverse, w * inverse))

    for side in range(2):
        wait_y(side, yrecv0.at[side, pl.ds(2 * nx, 2 * nx)], 1)
    for side in range(2):
        for f in range(2):
            value = yrecv0[side, (2 + f) * nx : (3 + f) * nx]
            kept, scale = fresh_parts[2 * side + f]
            fresh = kept + scale * value
            state.at[1, f][edge_row[side], :] = fresh
            ysend[side, ONE, f * nx : (f + 1) * nx] = fresh
        send_y(ONE, side)
    for side in range(2):
        send_x(ONE, side, [state.at[1, f, edge_plane[side]] for f in range(2)])

    sweep(1)

    for f in range(2):
        for side in range(2):
            ysend[side, INV, f * nx : (f + 1) * nx] = inv.at[f][edge_row[side], :]
    for side in range(2):
        send_y(INV, side)
        send_x(INV, side, [inv.at[f, edge_plane[side]] for f in range(2)])

    for side in range(2):
        for f in range(2):
            cut = edge_plane[side]
            scale = inv[f, cut]
            inner = wx[f, plane(1) if side == 0 else plane(nx - 1)]
            parts = (
                force[f, cut],
                couple[f],
                wy[f, 0, cut],
                wy[f, 1, cut],
                inner,
                wz[f, 0, cut],
                wz[f, 1, cut],
                hwx[f, side],
            )
            for n, part in enumerate(parts):
                xface[side, f, n] = part * scale
            xface[side, f, 8] = inner * inv[f, next_plane[side]]

            cut = edge_row[side]
            scale = inv.at[f][cut, :]
            inner = wy.at[f, 1 - side][cut, :]
            parts = (
                force.at[f][cut, :],
                couple[f],
                wx.at[f][rows(side * (ny - 1)), :],
                wx.at[f][rows(side * (ny - 1), 1), :],
                inner,
                wz.at[f, 0][cut, :],
                wz.at[f, 1][cut, :],
                hwy[f, side],
            )
            for n, part in enumerate(parts):
                yface[side, f, n] = part * scale
            yface[side, f, 8] = inner * inv.at[f][next_row[side], :]

    at_low = lane % TILE == 0
    at_high = lane % TILE == TILE - 1

    @pl.loop(0, nx, unroll=8)
    def _(i):
        d = damage[at(i + 1)]
        low = jnp.where(at_low & (lane > 0), pltpu.roll(d, 1, 1), 0.0)
        high = jnp.where(at_high & (lane < nz - 1), pltpu.roll(d, nz - 1, 1), 0.0)
        around[at(i)] = low + high

    for side in range(2):
        around[edge_plane[side], :] = around[edge_plane[side], :] + xrecv0[side, 0:ny]
    for side in range(2):
        around[edge_row[side], :] = around[edge_row[side], :] + yrecv0[side, 0:nx]
    arrived(tough, in_sem.at[2])
    arrived(roster, in_sem.at[3])
    tile_of = lane // TILE
    chosen = tile_of == roster[0]
    for n in range(1, roster.shape[0]):
        chosen = chosen | (tile_of == roster[n])
    listed[...] = jnp.where(chosen, 1.0, 0.0)

    for side in range(2):
        wait_x(side, xrecv.at[side, ONE], 1)
    for side in range(2):
        cut = edge_plane[side]
        for f in range(2):
            value = xrecv[side, ONE, f * ny : (f + 1) * ny]
            state[2, f, cut] = state[2, f, cut] + xface[side, f, 7] * value
    for side in range(2):
        wait_y(side, yrecv.at[side, ONE], 2)
        for f in range(2):
            cut = edge_row[side]
            value = yrecv[side, ONE, f * nx : (f + 1) * nx]
            fresh = state.at[2, f][cut, :] + yface[side, f, 7] * value
            state.at[2, f][cut, :] = fresh
            ysend[side, TWO, f * nx : (f + 1) * nx] = fresh
        send_y(TWO, side)
    for side in range(2):
        send_x(TWO, side, [state.at[2, f, edge_plane[side]] for f in range(2)])

    def along(face, n, own):
        return (
            face[2] * pltpu.roll(own, 1, 0)
            + face[3] * pltpu.roll(own, n - 1, 0)
            + face[5] * pltpu.roll(own, 1, 1)
            + face[6] * pltpu.roll(own, nz - 1, 1)
        )

    for side in range(2):
        own = [ysend[side, TWO, f * nx : (f + 1) * nx] for f in range(2)]
        for f in range(2):
            face = yface.at[side, f]
            inner = state.at[2, f][next_row[side], :]
            value = face[0] + face[1] * own[1 - f] + face[4] * inner + along(face, nx, own[f])
            ysend[side, PART, f * nx : (f + 1) * nx] = value
        send_y(PART, side)

    for c, (sx, sy) in enumerate(corners):
        xe = sx * (nx - 1)
        ye = sy * (ny - 1)
        for f in range(2):
            value = state[2, f, pl.ds(xe * ny + ye, 1), :]
            csend[c, f : f + 1] = hwx[f, sx, ye : ye + 1] * value
            csend[c, 2 + f : 3 + f] = hwy[f, sy, xe : xe + 1] * value

        @pl.when(has_c[c])
        def _():
            remote(csend.at[c], crecv.at[3 - c], send_sem.at[4 + c], cr.at[3 - c], to_c[c]).start()

    for side in range(2):
        own = [state[2, f, edge_plane[side]] for f in range(2)]
        for f in range(2):
            face = xface.at[side, f]
            inner = state[2, f, next_plane[side]]
            value = face[0] + face[1] * own[1 - f] + face[4] * inner + along(face, ny, own[f])
            xsend[side, f] = value
        send_x(PART, side, [xsend.at[side, f] for f in range(2)])

    sweep(2)
    sweep(3)

    def ends(count, low, high):
        spot = lax.broadcasted_iota(jnp.int32, (count, nz), 0)
        return jnp.where(spot == 0, low, jnp.where(spot == count - 1, high, 0.0))

    for side in range(2):
        wait_x(side, xrecv.at[side, TWO], 2)
        wait_x(side, xrecv.at[side, pl.ds(PART, 2)], 3)
    for c in range(4):

        @pl.when(has_c[c])
        def _():
            arrived(crecv.at[c], cr.at[c])

    for side in range(2):
        cut = edge_plane[side]
        change = [
            xface[side, f, 7] * xrecv[side, TWO, f * ny : (f + 1) * ny] for f in range(2)
        ]
        for f in range(2):
            face = xface.at[side, f]
            both = slice(f * ny, (f + 1) * ny)
            more = ends(
                ny, crecv[2 * side, 2 + f : 3 + f], crecv[2 * side + 1, 2 + f : 3 + f]
            )
            beyond = xrecv[side, PART, both] + xrecv[side, INV, both] * (
                hwx[f, side] * state[2, f, cut] + more
            )
            add = face[1] * change[1 - f] + along(face, ny, change[f]) + face[7] * beyond
            final[f, cut] = final[f, cut] + add
            cut_in = next_plane[side]
            final[f, cut_in] = final[f, cut_in] + face[8] * change[f]

    for side in range(2):
        wait_y(side, yrecv.at[side, TWO], 3)
        cut = edge_row[side]
        cut_in = next_row[side]
        change = [
            yface[side, f, 7] * yrecv[side, TWO, f * nx : (f + 1) * nx] for f in range(2)
        ]
        adds = []
        for f in range(2):
            face = yface.at[side, f]
            final.at[f][cut_in, :] = final.at[f][cut_in, :] + face[8] * change[f]
            adds.append(
                final.at[f][cut, :] + face[1] * change[1 - f] + along(face, nx, change[f])
            )
        wait_y(side, yrecv.at[side, pl.ds(PART, 2)], 4)
        for f in range(2):
            both = slice(f * nx, (f + 1) * nx)
            more = ends(nx, crecv[side, f : f + 1], crecv[2 + side, f : f + 1])
            more = more + hwy[f, side] * ysend[side, TWO, both]
            beyond = yrecv[side, PART, both] + yrecv[side, INV, both] * more
            final.at[f][cut, :] = adds[f] + yface[side, f, 7] * beyond

    for c in range(4):

        @pl.when(has_c[c])
        def _():
            arrived(csend.at[c], send_sem.at[4 + c])

    for side in range(2):

        @pl.when(has_y[side])
        def _():
            arrived(fixed.at[0, pl.ds(0, (4 + 2 * SENDS) * nx)], send_sem.at[2 + side])

        @pl.when(has_x[side])
        def _():
            arrived(fixed.at[0, pl.ds(0, (4 + 2 * SENDS) * ny)], send_sem.at[side])


def finish(
    sizes,
    final,
    damage,
    around,
    tough,
    listed,
    p_out,
    t_out,
    d_out,
    work,
    da,
    db,
    out_sem,
):
    nx, ny, nz = sizes
    cells = nx * ny
    row = lax.broadcasted_iota(jnp.int32, (ny, nz), 0)
    lane = lax.broadcasted_iota(jnp.int32, (ny, nz), 1)

    def at(i):
        return pl.ds(pl.multiple_of(i * ny, ny), ny)

    outs = [
        pltpu.make_async_copy(final.at[0], p_out, out_sem.at[0]),
        pltpu.make_async_copy(final.at[1], t_out, out_sem.at[0]),
    ]
    for out in outs:
        out.start()

    zero_plane = jnp.zeros((ny, nz), F32)
    for which in range(2):
        work[which, 0:ny] = zero_plane
        work[which, (nx + 1) * ny : (nx + 2) * ny] = zero_plane

    y_first = row == 0
    y_last = row == ny - 1
    z_first = lane % TILE == 0
    z_last = lane % TILE == TILE - 1
    inside = listed[...] > 0.0

    piece = cells // CHUNKS
    last = [
        pltpu.make_async_copy(
            work.at[0, pl.ds(ny + chunk * piece, piece)],
            d_out.at[pl.ds(chunk * piece, piece)],
            out_sem.at[1],
        )
        for chunk in range(CHUNKS)
    ]
    for step in range(DAMAGE_SWEEPS):
        source = (damage, work.at[0], work.at[1])[step % 3]
        target = (work.at[0], work.at[1], work.at[0])[step % 3]

        def relax(i):
            d = source[at(i + 1)]
            near = around[at(i)] + source[at(i)] + source[at(i + 2)]
            near = near + jnp.where(y_first, 0.0, pltpu.roll(d, 1, 0))
            near = near + jnp.where(y_last, 0.0, pltpu.roll(d, ny - 1, 0))
            near = near + jnp.where(z_first, 0.0, pltpu.roll(d, 1, 1))
            near = near + jnp.where(z_last, 0.0, pltpu.roll(d, nz - 1, 1))
            if step == 0:
                load = final[0, at(i)]
                hard = tough[at(i)]
                drive = 2.0 * energy_scale * load * load
                spread = hard * crack_length
                inverse = 1.0 / (hard / crack_length + drive + 6.0 * spread)
                a = drive * inverse
                b = spread * inverse
                da[at(i)] = a
                db[at(i)] = b
            else:
                a = da[at(i)]
                b = db[at(i)]
            fresh = a + b * near
            if step == DAMAGE_SWEEPS - 1:
                fresh = jnp.where(inside, fresh, damage[at(i + 1)])
            target[at(i + 1)] = fresh

        if step < DAMAGE_SWEEPS - 1:
            pl.loop(0, nx, unroll=8)(relax)
        else:
            for chunk in range(CHUNKS):
                pl.loop(chunk * nx // CHUNKS, (chunk + 1) * nx // CHUNKS, unroll=8)(relax)
                last[chunk].start()

    pltpu.make_async_copy(final, final, out_sem.at[0]).wait()
    whole = work.at[0, pl.ds(ny, cells)]
    pltpu.make_async_copy(whole, whole, out_sem.at[1]).wait()


def body(counts, names, *arrays):
    nx, ny, nz = arrays[0].shape
    cells = nx * ny
    flat = [a.reshape(cells, nz) for a in arrays[:-1]] + [arrays[-1]]
    flat = [pltpu.with_memory_space_constraint(a, pltpu.HBM) for a in flat]
    block = jax.ShapeDtypeStruct((cells, nz), F32)
    dma = pltpu.SemaphoreType.DMA
    vmem = pl.BlockSpec(memory_space=pltpu.VMEM)
    hbm = pl.BlockSpec(memory_space=pl.ANY)
    middle = pl.pallas_call(
        functools.partial(kernel, names, (nx, ny, nz) + counts),
        out_shape=(
            jax.ShapeDtypeStruct((2, cells, nz), F32),
            jax.ShapeDtypeStruct((cells + 2 * ny, nz), F32),
            block,
            block,
            jax.ShapeDtypeStruct((ny, nz), F32),
        ),
        in_specs=[hbm] * 8,
        out_specs=[vmem] * 5,
        scratch_shapes=[
            pltpu.VMEM((SWEEPS, 2, cells, nz), F32),
            pltpu.VMEM((3, cells, nz), F32),
            pltpu.VMEM((2, cells, nz), F32),
            pltpu.VMEM((2, cells, nz), F32),
            pltpu.VMEM((2, cells + ny, nz), F32),
            pltpu.VMEM((2, 2, cells, nz), F32),
            pltpu.VMEM((2, 2, cells, nz), F32),
            pltpu.VMEM((2, cells, nz), F32),
            pltpu.VMEM((2, cells, nz), F32),
            pltpu.VMEM((2, 2, ny, nz), F32),
            pltpu.VMEM((2, 2, nx, nz), F32),
            pltpu.VMEM((2, 2, 9, ny, nz), F32),
            pltpu.VMEM((2, 2, 9, nx, nz), F32),
            pltpu.VMEM((2, 4 * nx, nz), F32),
            pltpu.VMEM((2, 4 * nx, nz), F32),
            pltpu.VMEM((2, 4 * ny, nz), F32),
            pltpu.VMEM((2, SENDS, 2 * nx, nz), F32),
            pltpu.VMEM((2, SENDS, 2 * nx, nz), F32),
            pltpu.VMEM((2, 2, ny, nz), F32),
            pltpu.VMEM((2, SENDS, 2 * ny, nz), F32),
            pltpu.VMEM((4, 8, nz), F32),
            pltpu.VMEM((4, 8, nz), F32),
            pltpu.SMEM(arrays[-1].shape, jnp.int32),
            dma((4,)),
            dma((8,)),
            dma((2, 4)),
            dma((2, 5)),
            dma((4,)),
        ],
        compiler_params=pltpu.CompilerParams(
            collective_id=0, has_side_effects=True, vmem_limit_bytes=40 * 2**20
        ),
    )(*flat)
    outs = pl.pallas_call(
        functools.partial(finish, (nx, ny, nz)),
        out_shape=(block, block, block),
        in_specs=[vmem] * 5,
        out_specs=[hbm] * 3,
        scratch_shapes=[
            pltpu.VMEM((2, cells + 2 * ny, nz), F32),
            pltpu.VMEM((cells, nz), F32),
            pltpu.VMEM((cells, nz), F32),
            dma((2,)),
        ],
        compiler_params=pltpu.CompilerParams(vmem_limit_bytes=16 * 2**20),
    )(*middle)
    return tuple(o.reshape(nx, ny, nz) for o in outs)


def solution(mesh):
    cut = P("gx", "gy", None)
    names = ("gx", "gy")
    counts = (mesh.shape["gx"], mesh.shape["gy"])
    return jax.shard_map(
        functools.partial(body, counts, names),
        mesh=mesh,
        in_specs=(cut,) * 7 + (P(("gx", "gy")),),
        out_specs=(cut, cut, cut),
        check_vma=False,
    )
```

```python
import functools

import jax
import jax.numpy as jnp
from jax import lax
from jax.experimental import pallas as pl
from jax.experimental.pallas import tpu as pltpu
from jax.sharding import PartitionSpec as P

TILE = 32
SWEEPS = 4
DAMAGE_SWEEPS = 3
CHUNKS = 4
ONE, TWO, PART, INV = range(4)
OWN, DEN, Y_TWO, Y_PART = range(4)
SENDS = 4

capacity = (0.5, 0.5)
couple = (0.3, 0.3)
residual_open = 0.05
harmonic_floor = 0.001
crack_length = 2.0
energy_scale = 2.0
F32 = jnp.float32


def harmonic(left, right):
    return 2.0 * left * right / (left + right + harmonic_floor)


def kernel(
    names,
    sizes,
    p_hbm,
    t_hbm,
    d_hbm,
    k_hbm,
    g_hbm,
    qp_hbm,
    qt_hbm,
    roster_hbm,
    final,
    damage,
    around,
    tough,
    listed,
    state,
    fixed,
    force,
    conduct,
    wx,
    wy,
    wz,
    den,
    inv,
    hwx,
    hwy,
    xface,
    yface,
    ysend0,
    yrecv0,
    xrecv0,
    ysend,
    yrecv,
    xsend,
    xrecv,
    csend,
    crecv,
    known,
    yinv,
    roster,
    in_sem,
    send_sem,
    xr,
    yr,
    cr,
):
    nx, ny, nz, count_x, count_y = sizes
    cells = nx * ny
    gx, gy = names
    ix = lax.axis_index(gx)
    iy = lax.axis_index(gy)
    has_x = (ix > 0, ix < count_x - 1)
    has_y = (iy > 0, iy < count_y - 1)
    to_x = ({gx: ix - 1}, {gx: ix + 1})
    to_y = ({gy: iy - 1}, {gy: iy + 1})
    corners = [(sx, sy) for sx in range(2) for sy in range(2)]
    has_c = [has_x[sx] & has_y[sy] for sx, sy in corners]
    to_c = [to_x[sx] | to_y[sy] for sx, sy in corners]
    mesh_type = pl.DeviceIdType.MESH

    barrier = pltpu.get_barrier_semaphore()
    for has, to in ((has_y, to_y), (has_x, to_x)):
        for side in range(2):

            @pl.when(has[side])
            def _():
                pl.semaphore_signal(barrier, inc=1, device_id=to[side], device_id_type=mesh_type)

    load = pltpu.make_async_copy
    first = [
        load(d_hbm, damage.at[pl.ds(ny, cells)], in_sem.at[0]),
        load(k_hbm, fixed.at[0], in_sem.at[0]),
        load(p_hbm, state.at[0, 0], in_sem.at[0]),
        load(t_hbm, state.at[0, 1], in_sem.at[0]),
    ]
    rates = [
        load(qp_hbm, fixed.at[1], in_sem.at[1]),
        load(qt_hbm, fixed.at[2], in_sem.at[1]),
    ]
    late = [
        load(g_hbm, tough, in_sem.at[2]),
        load(roster_hbm, roster, in_sem.at[3]),
    ]
    for copy in first + rates + late:
        copy.start()

    def arrived(ref, sem):
        pltpu.make_async_copy(ref, ref, sem).wait()

    csend[...] = jnp.zeros(csend.shape, F32)
    for c in range(4):

        @pl.when(jnp.logical_not(has_c[c]))
        def _():
            crecv[c] = jnp.zeros(crecv.shape[1:], F32)

    for side in range(2):

        @pl.when(jnp.logical_not(has_x[side]))
        def _():
            xrecv0[side] = jnp.zeros(xrecv0.shape[1:], F32)
            for step in range(SENDS):
                xrecv[side, step] = jnp.zeros(xrecv.shape[2:], F32)

        @pl.when(jnp.logical_not(has_y[side]))
        def _():
            yrecv0[side] = jnp.zeros(yrecv0.shape[1:], F32)
            for step in range(SENDS):
                yrecv[side, step] = jnp.full(yrecv.shape[2:], float(step == DEN), F32)

    zero_plane = jnp.zeros((ny, nz), F32)
    damage[0:ny] = zero_plane
    damage[(nx + 1) * ny : (nx + 2) * ny] = zero_plane
    for f in range(2):
        wx[f, 0:ny] = zero_plane
        wx[f, nx * ny : (nx + 1) * ny] = zero_plane

    def rows(r, first_plane=0):
        return pl.ds(first_plane * ny + r, nx, stride=ny)

    def plane(i):
        return pl.ds(i * ny, ny)

    edge_row = (rows(0), rows(ny - 1))
    next_row = (rows(1), rows(ny - 2))
    edge_plane = (plane(0), plane(nx - 1))
    next_plane = (plane(1), plane(nx - 2))
    edge_pad = (rows(0, 1), rows(ny - 1, 1))
    edge_plane_pad = (plane(1), plane(nx))

    arrived(state.at[pl.ds(0, 2)], in_sem.at[0])

    for side in range(2):
        ysend0[side, 0 * nx : 1 * nx] = damage[edge_pad[side], :]
        ysend0[side, 1 * nx : 2 * nx] = fixed.at[0][edge_row[side], :]
        ysend0[side, 2 * nx : 3 * nx] = state.at[0, 0][edge_row[side], :]
        ysend0[side, 3 * nx : 4 * nx] = state.at[0, 1][edge_row[side], :]

    def remote(source, target, send, recv, to):
        return pltpu.make_async_remote_copy(
            src_ref=source,
            dst_ref=target,
            send_sem=send,
            recv_sem=recv,
            device_id=to,
            device_id_type=mesh_type,
        )

    place = {ONE: 1, TWO: 2, PART: 3, INV: 3}

    def send_y(step, count, side):
        @pl.when(has_y[side])
        def _():
            remote(
                ysend.at[side, pl.ds(step, count)],
                yrecv.at[1 - side, pl.ds(step, count)],
                send_sem.at[2 + side],
                yr.at[1 - side, {OWN: 2, Y_TWO: 3, Y_PART: 4}[step]],
                to_y[side],
            ).start()

    def send_x(step, side, sources):
        @pl.when(has_x[side])
        def _():
            for f in range(2):
                remote(
                    sources[f],
                    xrecv.at[1 - side, step, pl.ds(f * ny, ny)],
                    send_sem.at[side],
                    xr.at[1 - side, place[step]],
                    to_x[side],
                ).start()

    def wait_y(side, ref, n):
        @pl.when(has_y[side])
        def _():
            arrived(ref, yr.at[side, n])

    def wait_x(side, ref, n):
        @pl.when(has_x[side])
        def _():
            arrived(ref, xr.at[side, n])

    peers = sum(jnp.where(has, 1, 0).astype(jnp.int32) for has in has_x + has_y)
    pl.semaphore_wait(barrier, peers)

    for half in range(2):
        for side in range(2):

            @pl.when(has_y[side])
            def _():
                part = pl.ds(half * 2 * nx, 2 * nx)
                remote(
                    ysend0.at[side, part],
                    yrecv0.at[1 - side, part],
                    send_sem.at[2 + side],
                    yr.at[1 - side, half],
                    to_y[side],
                ).start()

    for side in range(2):
        sources = (
            damage.at[edge_plane_pad[side]],
            fixed.at[0, edge_plane[side]],
            state.at[0, 0, edge_plane[side]],
            state.at[0, 1, edge_plane[side]],
        )

        @pl.when(has_x[side])
        def _():
            for n, source in enumerate(sources):
                remote(
                    source,
                    xrecv0.at[1 - side, pl.ds(n * ny, ny)],
                    send_sem.at[side],
                    xr.at[1 - side, 0],
                    to_x[side],
                ).start()

    row = lax.broadcasted_iota(jnp.int32, (ny, nz), 0)
    lane = lax.broadcasted_iota(jnp.int32, (ny, nz), 1)

    def at(i):
        return pl.ds(pl.multiple_of(i * ny, ny), ny)

    def open_of(d):
        return (1.0 - d) * (1.0 - d) + residual_open

    arrived(fixed.at[pl.ds(1, 2)], in_sem.at[1])

    @pl.loop(0, nx, unroll=8)
    def _(i):
        openness = open_of(damage[at(i + 1)])
        conduct[1, at(i)] = openness
        conduct[0, at(i)] = fixed[0, at(i)] * openness
        for f in range(2):
            force[f, at(i)] = fixed[1 + f, at(i)] + capacity[f] * state[0, f, at(i)]

    @pl.loop(0, nx, unroll=8)
    def _(i):
        follow = jnp.minimum(i + 1, nx - 1)
        inside = jnp.where(i < nx - 1, 1.0, 0.0).astype(F32)
        for f in range(2):
            own = conduct[f, at(i)]
            ahead = harmonic(own, conduct[f, at(follow)]) * inside
            wx[f, at(i + 1)] = ahead
            y_hi = jnp.where(row < ny - 1, harmonic(own, pltpu.roll(own, ny - 1, 0)), 0.0)
            y_lo = pltpu.roll(y_hi, 1, 0)
            z_hi = jnp.where(lane < nz - 1, harmonic(own, pltpu.roll(own, nz - 1, 1)), 0.0)
            z_lo = pltpu.roll(z_hi, 1, 1)
            wy[f, 0, at(i)] = y_lo
            wy[f, 1, at(i)] = y_hi
            wz[f, 0, at(i)] = z_lo
            wz[f, 1, at(i)] = z_hi
            total = capacity[f] + ahead + wx[f, at(i)] + y_lo + y_hi + z_lo + z_hi
            den[f, at(i)] = total
            inv[f, at(i)] = 1.0 / total

    levels = [state.at[step] for step in range(SWEEPS)] + [final]

    def sweep(step, start=0, stop=nx):
        @pl.loop(start, stop, unroll=8)
        def _(i):
            before = jnp.maximum(i - 1, 0)
            follow = jnp.minimum(i + 1, nx - 1)
            center = [state[step, f, at(i)] for f in range(2)]
            for f in range(2):
                c = center[f]
                acc = force[f, at(i)] + couple[f] * center[1 - f]
                acc = acc + wx[f, at(i)] * state[step, f, at(before)]
                acc = acc + wx[f, at(i + 1)] * state[step, f, at(follow)]
                acc = acc + wy[f, 0, at(i)] * pltpu.roll(c, 1, 0)
                acc = acc + wy[f, 1, at(i)] * pltpu.roll(c, ny - 1, 0)
                acc = acc + wz[f, 0, at(i)] * pltpu.roll(c, 1, 1)
                acc = acc + wz[f, 1, at(i)] * pltpu.roll(c, nz - 1, 1)
                levels[step + 1][f, at(i)] = acc * inv[f, at(i)]

    for side in range(2):
        wait_x(side, xrecv0.at[side], 0)

    for side in range(2):
        there = jnp.where(has_x[side], 1.0, 0.0).astype(F32)
        openness = open_of(xrecv0[side, 0:ny]) * there
        halo_conduct = (xrecv0[side, ny : 2 * ny] * openness, openness)
        for f in range(2):
            hwx[f, side] = harmonic(conduct[f, edge_plane[side]], halo_conduct[f])

    def ends(count, low, high):
        spot = lax.broadcasted_iota(jnp.int32, (count, nz), 0)
        return jnp.where(spot == 0, low, jnp.where(spot == count - 1, high, 0.0))

    sweep(0)

    for side in range(2):
        cut = edge_row[side]
        r = side * (ny - 1)
        own = [ysend0[side, (2 + f) * nx : (3 + f) * nx] for f in range(2)]
        for f in range(2):
            both = slice(f * nx, (f + 1) * nx)
            weight = [hwx[f, sx, r : r + 1] for sx in range(2)]
            flow = [
                weight[sx] * xrecv0[sx, (2 + f) * ny + r : (2 + f) * ny + r + 1] for sx in range(2)
            ]
            ysend[side, DEN, both] = den.at[f][cut, :] + ends(nx, *weight)
            ysend[side, OWN, both] = (
                force.at[f][cut, :]
                + couple[f] * own[1 - f]
                + wx.at[f][rows(r), :] * pltpu.roll(own[f], 1, 0)
                + wx.at[f][rows(r, 1), :] * pltpu.roll(own[f], nx - 1, 0)
                + wy.at[f, 1 - side][cut, :] * state.at[0, f][next_row[side], :]
                + wz.at[f, 0][cut, :] * pltpu.roll(own[f], 1, 1)
                + wz.at[f, 1][cut, :] * pltpu.roll(own[f], nz - 1, 1)
                + ends(nx, *flow)
            )
        send_y(OWN, 2, side)

    for side in range(2):
        cut = edge_plane[side]
        for f in range(2):
            w = hwx[f, side]
            old = den[f, cut]
            total = old + w
            inverse = 1.0 / total
            den[f, cut] = total
            inv[f, cut] = inverse
            value = xrecv0[side, (2 + f) * ny : (3 + f) * ny]
            state[1, f, cut] = (state[1, f, cut] * old + w * value) * inverse

    for side in range(2):
        wait_y(side, yrecv0.at[side, pl.ds(0, 2 * nx)], 0)
        wait_y(side, yrecv0.at[side, pl.ds(2 * nx, 2 * nx)], 1)

    for side in range(2):
        there = jnp.where(has_y[side], 1.0, 0.0).astype(F32)
        openness = open_of(yrecv0[side, 0:nx]) * there
        halo_conduct = (yrecv0[side, nx : 2 * nx] * openness, openness)
        cut = edge_row[side]
        for f in range(2):
            w = harmonic(conduct.at[f][cut, :], halo_conduct[f])
            hwy[f, side] = w
            old = den.at[f][cut, :]
            inverse = 1.0 / (old + w)
            inv.at[f][cut, :] = inverse
            known[side, f] = w * ysend0[side, (2 + f) * nx : (3 + f) * nx]
            value = yrecv0[side, (2 + f) * nx : (3 + f) * nx]
            state.at[1, f][cut, :] = (state.at[1, f][cut, :] * old + w * value) * inverse
    for side in range(2):
        send_x(ONE, side, [state.at[1, f, edge_plane[side]] for f in range(2)])

    sweep(1)

    for side in range(2):
        send_x(INV, side, [inv.at[f, edge_plane[side]] for f in range(2)])

    for side in range(2):
        for f in range(2):
            cut = edge_plane[side]
            scale = inv[f, cut]
            inner = wx[f, plane(1) if side == 0 else plane(nx - 1)]
            parts = (
                force[f, cut],
                couple[f],
                wy[f, 0, cut],
                wy[f, 1, cut],
                inner,
                wz[f, 0, cut],
                wz[f, 1, cut],
                hwx[f, side],
            )
            for n, part in enumerate(parts):
                xface[side, f, n] = part * scale
            xface[side, f, 8] = inner * inv[f, next_plane[side]]

            cut = edge_row[side]
            scale = inv.at[f][cut, :]
            inner = wy.at[f, 1 - side][cut, :]
            parts = (
                force.at[f][cut, :],
                couple[f],
                wx.at[f][rows(side * (ny - 1)), :],
                wx.at[f][rows(side * (ny - 1), 1), :],
                inner,
                wz.at[f, 0][cut, :],
                wz.at[f, 1][cut, :],
                hwy[f, side],
            )
            for n, part in enumerate(parts):
                yface[side, f, n] = part * scale
            yface[side, f, 8] = inner * inv.at[f][next_row[side], :]

    at_low = lane % TILE == 0
    at_high = lane % TILE == TILE - 1

    @pl.loop(0, nx, unroll=8)
    def _(i):
        d = damage[at(i + 1)]
        low = jnp.where(at_low & (lane > 0), pltpu.roll(d, 1, 1), 0.0)
        high = jnp.where(at_high & (lane < nz - 1), pltpu.roll(d, nz - 1, 1), 0.0)
        around[at(i)] = low + high

    for side in range(2):
        around[edge_plane[side], :] = around[edge_plane[side], :] + xrecv0[side, 0:ny]
    for side in range(2):
        around[edge_row[side], :] = around[edge_row[side], :] + yrecv0[side, 0:nx]
    arrived(tough, in_sem.at[2])
    arrived(roster, in_sem.at[3])
    tile_of = lane // TILE
    chosen = tile_of == roster[0]
    for n in range(1, roster.shape[0]):
        chosen = chosen | (tile_of == roster[n])
    listed[...] = jnp.where(chosen, 1.0, 0.0)

    def along(face, n, own):
        return (
            face[2] * pltpu.roll(own, 1, 0)
            + face[3] * pltpu.roll(own, n - 1, 0)
            + face[5] * pltpu.roll(own, 1, 1)
            + face[6] * pltpu.roll(own, nz - 1, 1)
        )

    for side in range(2):
        wait_x(side, xrecv.at[side, ONE], 1)
    for side in range(2):
        cut = edge_plane[side]
        for f in range(2):
            value = xrecv[side, ONE, f * ny : (f + 1) * ny]
            state[2, f, cut] = state[2, f, cut] + xface[side, f, 7] * value
    for side in range(2):
        wait_y(side, yrecv.at[side, pl.ds(OWN, 2)], 2)
        for f in range(2):
            cut = edge_row[side]
            both = slice(f * nx, (f + 1) * nx)
            inverse = 1.0 / (yrecv[side, DEN, both] + hwy[f, side])
            yinv[side, f] = inverse
            value = (yrecv[side, OWN, both] + known[side, f]) * inverse
            fresh = state.at[2, f][cut, :] + yface[side, f, 7] * value
            state.at[2, f][cut, :] = fresh
            ysend[side, Y_TWO, both] = fresh
        send_y(Y_TWO, 1, side)
        own = [ysend[side, Y_TWO, f * nx : (f + 1) * nx] for f in range(2)]
        for f in range(2):
            face = yface.at[side, f]
            inner = state.at[2, f][next_row[side], :]
            value = face[0] + face[1] * own[1 - f] + face[4] * inner + along(face, nx, own[f])
            ysend[side, Y_PART, f * nx : (f + 1) * nx] = value
        send_y(Y_PART, 1, side)
    for side in range(2):
        send_x(TWO, side, [state.at[2, f, edge_plane[side]] for f in range(2)])

    for c, (sx, sy) in enumerate(corners):
        xe = sx * (nx - 1)
        ye = sy * (ny - 1)
        for f in range(2):
            value = state[2, f, pl.ds(xe * ny + ye, 1), :]
            csend[c, f : f + 1] = hwx[f, sx, ye : ye + 1] * value
            csend[c, 2 + f : 3 + f] = hwy[f, sy, xe : xe + 1] * value

        @pl.when(has_c[c])
        def _():
            remote(csend.at[c], crecv.at[3 - c], send_sem.at[4 + c], cr.at[3 - c], to_c[c]).start()

    for side in range(2):
        own = [state[2, f, edge_plane[side]] for f in range(2)]
        for f in range(2):
            face = xface.at[side, f]
            inner = state[2, f, next_plane[side]]
            value = face[0] + face[1] * own[1 - f] + face[4] * inner + along(face, ny, own[f])
            xsend[side, f] = value
        send_x(PART, side, [xsend.at[side, f] for f in range(2)])

    sweep(2)
    sweep(3)

    for side in range(2):
        wait_x(side, xrecv.at[side, TWO], 2)
    for side in range(2):
        cut = edge_plane[side]
        cut_in = next_plane[side]
        change = [
            xface[side, f, 7] * xrecv[side, TWO, f * ny : (f + 1) * ny] for f in range(2)
        ]
        for f in range(2):
            face = xface.at[side, f]
            add = face[1] * change[1 - f] + along(face, ny, change[f])
            final[f, cut] = final[f, cut] + add
            final[f, cut_in] = final[f, cut_in] + face[8] * change[f]

    for side in range(2):
        wait_y(side, yrecv.at[side, Y_TWO], 3)
        cut = edge_row[side]
        cut_in = next_row[side]
        change = [
            yface[side, f, 7] * yrecv[side, Y_TWO, f * nx : (f + 1) * nx] for f in range(2)
        ]
        for f in range(2):
            face = yface.at[side, f]
            add = face[1] * change[1 - f] + along(face, nx, change[f])
            final.at[f][cut, :] = final.at[f][cut, :] + add
            final.at[f][cut_in, :] = final.at[f][cut_in, :] + face[8] * change[f]

    for side in range(2):
        wait_x(side, xrecv.at[side, pl.ds(PART, 2)], 3)
    for c in range(4):

        @pl.when(has_c[c])
        def _():
            arrived(crecv.at[c], cr.at[c])

    for side in range(2):
        cut = edge_plane[side]
        for f in range(2):
            both = slice(f * ny, (f + 1) * ny)
            more = ends(
                ny, crecv[2 * side, 2 + f : 3 + f], crecv[2 * side + 1, 2 + f : 3 + f]
            )
            beyond = xrecv[side, PART, both] + xrecv[side, INV, both] * (
                hwx[f, side] * state[2, f, cut] + more
            )
            final[f, cut] = final[f, cut] + xface[side, f, 7] * beyond

    for side in range(2):
        wait_y(side, yrecv.at[side, Y_PART], 4)
        cut = edge_row[side]
        for f in range(2):
            both = slice(f * nx, (f + 1) * nx)
            more = ends(nx, crecv[side, f : f + 1], crecv[2 + side, f : f + 1])
            more = more + hwy[f, side] * ysend[side, Y_TWO, both]
            beyond = yrecv[side, Y_PART, both] + yinv[side, f] * more
            final.at[f][cut, :] = final.at[f][cut, :] + yface[side, f, 7] * beyond

    for c in range(4):

        @pl.when(has_c[c])
        def _():
            arrived(csend.at[c], send_sem.at[4 + c])

    for side in range(2):

        @pl.when(has_y[side])
        def _():
            arrived(fixed.at[0, pl.ds(0, (4 + 2 * SENDS) * nx)], send_sem.at[2 + side])

        @pl.when(has_x[side])
        def _():
            arrived(fixed.at[0, pl.ds(0, (4 + 2 * SENDS) * ny)], send_sem.at[side])


def finish(
    sizes,
    final,
    damage,
    around,
    tough,
    listed,
    p_out,
    t_out,
    d_out,
    work,
    da,
    db,
    out_sem,
):
    nx, ny, nz = sizes
    cells = nx * ny
    row = lax.broadcasted_iota(jnp.int32, (ny, nz), 0)
    lane = lax.broadcasted_iota(jnp.int32, (ny, nz), 1)

    def at(i):
        return pl.ds(pl.multiple_of(i * ny, ny), ny)

    outs = [
        pltpu.make_async_copy(final.at[0], p_out, out_sem.at[0]),
        pltpu.make_async_copy(final.at[1], t_out, out_sem.at[0]),
    ]
    for out in outs:
        out.start()

    zero_plane = jnp.zeros((ny, nz), F32)
    for which in range(2):
        work[which, 0:ny] = zero_plane
        work[which, (nx + 1) * ny : (nx + 2) * ny] = zero_plane

    y_first = row == 0
    y_last = row == ny - 1
    z_first = lane % TILE == 0
    z_last = lane % TILE == TILE - 1
    inside = listed[...] > 0.0

    piece = cells // CHUNKS
    last = [
        pltpu.make_async_copy(
            work.at[0, pl.ds(ny + chunk * piece, piece)],
            d_out.at[pl.ds(chunk * piece, piece)],
            out_sem.at[1],
        )
        for chunk in range(CHUNKS)
    ]
    for step in range(DAMAGE_SWEEPS):
        source = (damage, work.at[0], work.at[1])[step % 3]
        target = (work.at[0], work.at[1], work.at[0])[step % 3]

        def relax(i):
            d = source[at(i + 1)]
            near = around[at(i)] + source[at(i)] + source[at(i + 2)]
            near = near + jnp.where(y_first, 0.0, pltpu.roll(d, 1, 0))
            near = near + jnp.where(y_last, 0.0, pltpu.roll(d, ny - 1, 0))
            near = near + jnp.where(z_first, 0.0, pltpu.roll(d, 1, 1))
            near = near + jnp.where(z_last, 0.0, pltpu.roll(d, nz - 1, 1))
            if step == 0:
                load = final[0, at(i)]
                hard = tough[at(i)]
                drive = 2.0 * energy_scale * load * load
                spread = hard * crack_length
                inverse = 1.0 / (hard / crack_length + drive + 6.0 * spread)
                a = drive * inverse
                b = spread * inverse
                da[at(i)] = a
                db[at(i)] = b
            else:
                a = da[at(i)]
                b = db[at(i)]
            fresh = a + b * near
            if step == DAMAGE_SWEEPS - 1:
                fresh = jnp.where(inside, fresh, damage[at(i + 1)])
            target[at(i + 1)] = fresh

        if step < DAMAGE_SWEEPS - 1:
            pl.loop(0, nx, unroll=8)(relax)
        else:
            for chunk in range(CHUNKS):
                pl.loop(chunk * nx // CHUNKS, (chunk + 1) * nx // CHUNKS, unroll=8)(relax)
                last[chunk].start()

    pltpu.make_async_copy(final, final, out_sem.at[0]).wait()
    whole = work.at[0, pl.ds(ny, cells)]
    pltpu.make_async_copy(whole, whole, out_sem.at[1]).wait()


def body(counts, names, *arrays):
    nx, ny, nz = arrays[0].shape
    cells = nx * ny
    flat = [a.reshape(cells, nz) for a in arrays[:-1]] + [arrays[-1]]
    flat = [pltpu.with_memory_space_constraint(a, pltpu.HBM) for a in flat]
    block = jax.ShapeDtypeStruct((cells, nz), F32)
    dma = pltpu.SemaphoreType.DMA
    vmem = pl.BlockSpec(memory_space=pltpu.VMEM)
    hbm = pl.BlockSpec(memory_space=pl.ANY)
    middle = pl.pallas_call(
        functools.partial(kernel, names, (nx, ny, nz) + counts),
        out_shape=(
            jax.ShapeDtypeStruct((2, cells, nz), F32),
            jax.ShapeDtypeStruct((cells + 2 * ny, nz), F32),
            block,
            block,
            jax.ShapeDtypeStruct((ny, nz), F32),
        ),
        in_specs=[hbm] * 8,
        out_specs=[vmem] * 5,
        scratch_shapes=[
            pltpu.VMEM((SWEEPS, 2, cells, nz), F32),
            pltpu.VMEM((3, cells, nz), F32),
            pltpu.VMEM((2, cells, nz), F32),
            pltpu.VMEM((2, cells, nz), F32),
            pltpu.VMEM((2, cells + ny, nz), F32),
            pltpu.VMEM((2, 2, cells, nz), F32),
            pltpu.VMEM((2, 2, cells, nz), F32),
            pltpu.VMEM((2, cells, nz), F32),
            pltpu.VMEM((2, cells, nz), F32),
            pltpu.VMEM((2, 2, ny, nz), F32),
            pltpu.VMEM((2, 2, nx, nz), F32),
            pltpu.VMEM((2, 2, 9, ny, nz), F32),
            pltpu.VMEM((2, 2, 9, nx, nz), F32),
            pltpu.VMEM((2, 4 * nx, nz), F32),
            pltpu.VMEM((2, 4 * nx, nz), F32),
            pltpu.VMEM((2, 4 * ny, nz), F32),
            pltpu.VMEM((2, SENDS, 2 * nx, nz), F32),
            pltpu.VMEM((2, SENDS, 2 * nx, nz), F32),
            pltpu.VMEM((2, 2, ny, nz), F32),
            pltpu.VMEM((2, SENDS, 2 * ny, nz), F32),
            pltpu.VMEM((4, 8, nz), F32),
            pltpu.VMEM((4, 8, nz), F32),
            pltpu.VMEM((2, 2, nx, nz), F32),
            pltpu.VMEM((2, 2, nx, nz), F32),
            pltpu.SMEM(arrays[-1].shape, jnp.int32),
            dma((4,)),
            dma((8,)),
            dma((2, 4)),
            dma((2, 5)),
            dma((4,)),
        ],
        compiler_params=pltpu.CompilerParams(
            collective_id=0, has_side_effects=True, vmem_limit_bytes=40 * 2**20
        ),
    )(*flat)
    outs = pl.pallas_call(
        functools.partial(finish, (nx, ny, nz)),
        out_shape=(block, block, block),
        in_specs=[vmem] * 5,
        out_specs=[hbm] * 3,
        scratch_shapes=[
            pltpu.VMEM((2, cells + 2 * ny, nz), F32),
            pltpu.VMEM((cells, nz), F32),
            pltpu.VMEM((cells, nz), F32),
            dma((2,)),
        ],
        compiler_params=pltpu.CompilerParams(vmem_limit_bytes=16 * 2**20),
    )(*middle)
    return tuple(o.reshape(nx, ny, nz) for o in outs)


def solution(mesh):
    cut = P("gx", "gy", None)
    names = ("gx", "gy")
    counts = (mesh.shape["gx"], mesh.shape["gy"])
    return jax.shard_map(
        functools.partial(body, counts, names),
        mesh=mesh,
        in_specs=(cut,) * 7 + (P(("gx", "gy")),),
        out_specs=(cut, cut, cut),
        check_vma=False,
    )
```

```python
import functools

import jax
import jax.numpy as jnp
from jax import lax
from jax.experimental import pallas as pl
from jax.experimental.pallas import tpu as pltpu
from jax.sharding import PartitionSpec as P

TILE = 32
SWEEPS = 4
DAMAGE_SWEEPS = 3
CHUNKS = 4
ONE, TWO, PART, INV = range(4)
OWN, DEN, Y_TWO, Y_PART = range(4)
SENDS = 4

capacity = (0.5, 0.5)
couple = (0.3, 0.3)
residual_open = 0.05
harmonic_floor = 0.001
crack_length = 2.0
energy_scale = 2.0
F32 = jnp.float32


def harmonic(left, right):
    return 2.0 * left * right / (left + right + harmonic_floor)


def kernel(
    names,
    sizes,
    p_hbm,
    t_hbm,
    d_hbm,
    k_hbm,
    g_hbm,
    qp_hbm,
    qt_hbm,
    roster_hbm,
    final,
    damage,
    around,
    tough,
    listed,
    state0,
    state1,
    state2,
    state3,
    fixed,
    force,
    conduct,
    wx,
    wy,
    wz,
    den,
    inv,
    hwx,
    hwy,
    xface,
    yface,
    ysend0,
    yrecv0,
    xrecv0,
    ysend,
    yrecv,
    xsend,
    xrecv,
    csend,
    crecv,
    known,
    yinv,
    roster,
    in_sem,
    send_sem,
    xr,
    yr,
    cr,
):
    nx, ny, nz, count_x, count_y = sizes
    cells = nx * ny
    state = (state0, state1, state2, state3)
    gx, gy = names
    ix = lax.axis_index(gx)
    iy = lax.axis_index(gy)
    has_x = (ix > 0, ix < count_x - 1)
    has_y = (iy > 0, iy < count_y - 1)
    to_x = ({gx: ix - 1}, {gx: ix + 1})
    to_y = ({gy: iy - 1}, {gy: iy + 1})
    corners = [(sx, sy) for sx in range(2) for sy in range(2)]
    has_c = [has_x[sx] & has_y[sy] for sx, sy in corners]
    to_c = [to_x[sx] | to_y[sy] for sx, sy in corners]
    mesh_type = pl.DeviceIdType.MESH

    barrier = pltpu.get_barrier_semaphore()
    for has, to in ((has_y, to_y), (has_x, to_x)):
        for side in range(2):

            @pl.when(has[side])
            def _():
                pl.semaphore_signal(barrier, inc=1, device_id=to[side], device_id_type=mesh_type)

    load = pltpu.make_async_copy
    first = [
        load(d_hbm, damage.at[pl.ds(ny, cells)], in_sem.at[0]),
        load(k_hbm, fixed.at[0], in_sem.at[0]),
        load(p_hbm, state[0].at[0], in_sem.at[0]),
        load(t_hbm, state[0].at[1], in_sem.at[0]),
    ]
    rates = [
        load(qp_hbm, fixed.at[1], in_sem.at[1]),
        load(qt_hbm, fixed.at[2], in_sem.at[1]),
    ]
    late = [
        load(g_hbm, tough, in_sem.at[2]),
        load(roster_hbm, roster, in_sem.at[3]),
    ]
    for copy in first + rates + late:
        copy.start()

    def arrived(ref, sem):
        pltpu.make_async_copy(ref, ref, sem).wait()

    csend[...] = jnp.zeros(csend.shape, F32)
    for c in range(4):

        @pl.when(jnp.logical_not(has_c[c]))
        def _():
            crecv[c] = jnp.zeros(crecv.shape[1:], F32)

    for side in range(2):

        @pl.when(jnp.logical_not(has_x[side]))
        def _():
            xrecv0[side] = jnp.zeros(xrecv0.shape[1:], F32)
            for step in range(SENDS):
                xrecv[side, step] = jnp.zeros(xrecv.shape[2:], F32)

        @pl.when(jnp.logical_not(has_y[side]))
        def _():
            yrecv0[side] = jnp.zeros(yrecv0.shape[1:], F32)
            for step in range(SENDS):
                yrecv[side, step] = jnp.full(yrecv.shape[2:], float(step == DEN), F32)

    zero_plane = jnp.zeros((ny, nz), F32)
    damage[0:ny] = zero_plane
    damage[(nx + 1) * ny : (nx + 2) * ny] = zero_plane
    for f in range(2):
        wx[f, 0:ny] = zero_plane
        wx[f, nx * ny : (nx + 1) * ny] = zero_plane

    def rows(r, first_plane=0):
        return pl.ds(first_plane * ny + r, nx, stride=ny)

    def plane(i):
        return pl.ds(i * ny, ny)

    edge_row = (rows(0), rows(ny - 1))
    next_row = (rows(1), rows(ny - 2))
    edge_plane = (plane(0), plane(nx - 1))
    next_plane = (plane(1), plane(nx - 2))
    edge_pad = (rows(0, 1), rows(ny - 1, 1))
    edge_plane_pad = (plane(1), plane(nx))

    arrived(wy, in_sem.at[0])

    for side in range(2):
        ysend0[side, 0 * nx : 1 * nx] = damage[edge_pad[side], :]
        ysend0[side, 1 * nx : 2 * nx] = fixed.at[0][edge_row[side], :]
        ysend0[side, 2 * nx : 3 * nx] = state[0].at[0][edge_row[side], :]
        ysend0[side, 3 * nx : 4 * nx] = state[0].at[1][edge_row[side], :]

    def remote(source, target, send, recv, to):
        return pltpu.make_async_remote_copy(
            src_ref=source,
            dst_ref=target,
            send_sem=send,
            recv_sem=recv,
            device_id=to,
            device_id_type=mesh_type,
        )

    place = {ONE: 1, TWO: 2, PART: 3, INV: 3}

    def send_y(step, count, side):
        @pl.when(has_y[side])
        def _():
            remote(
                ysend.at[side, pl.ds(step, count)],
                yrecv.at[1 - side, pl.ds(step, count)],
                send_sem.at[2 + side],
                yr.at[1 - side, {OWN: 2, Y_TWO: 3, Y_PART: 4}[step]],
                to_y[side],
            ).start()

    def send_x(step, side, sources):
        @pl.when(has_x[side])
        def _():
            for f in range(2):
                remote(
                    sources[f],
                    xrecv.at[1 - side, step, pl.ds(f * ny, ny)],
                    send_sem.at[side],
                    xr.at[1 - side, place[step]],
                    to_x[side],
                ).start()

    def wait_y(side, ref, n):
        @pl.when(has_y[side])
        def _():
            arrived(ref, yr.at[side, n])

    def wait_x(side, ref, n):
        @pl.when(has_x[side])
        def _():
            arrived(ref, xr.at[side, n])

    peers = sum(jnp.where(has, 1, 0).astype(jnp.int32) for has in has_x + has_y)
    pl.semaphore_wait(barrier, peers)

    for half in range(2):
        for side in range(2):

            @pl.when(has_y[side])
            def _():
                part = pl.ds(half * 2 * nx, 2 * nx)
                remote(
                    ysend0.at[side, part],
                    yrecv0.at[1 - side, part],
                    send_sem.at[2 + side],
                    yr.at[1 - side, half],
                    to_y[side],
                ).start()

    for side in range(2):
        sources = (
            damage.at[edge_plane_pad[side]],
            fixed.at[0, edge_plane[side]],
            state[0].at[0, edge_plane[side]],
            state[0].at[1, edge_plane[side]],
        )

        @pl.when(has_x[side])
        def _():
            for n, source in enumerate(sources):
                remote(
                    source,
                    xrecv0.at[1 - side, pl.ds(n * ny, ny)],
                    send_sem.at[side],
                    xr.at[1 - side, 0],
                    to_x[side],
                ).start()

    row = lax.broadcasted_iota(jnp.int32, (ny, nz), 0)
    lane = lax.broadcasted_iota(jnp.int32, (ny, nz), 1)

    def at(i):
        return pl.ds(pl.multiple_of(i * ny, ny), ny)

    def open_of(d):
        return (1.0 - d) * (1.0 - d) + residual_open

    arrived(fixed.at[pl.ds(1, 2)], in_sem.at[1])

    @pl.loop(0, nx, unroll=8)
    def _(i):
        openness = open_of(damage[at(i + 1)])
        conduct[1, at(i)] = openness
        conduct[0, at(i)] = fixed[0, at(i)] * openness
        for f in range(2):
            force[f, at(i)] = fixed[1 + f, at(i)] + capacity[f] * state[0][f, at(i)]

    @pl.loop(0, nx, unroll=8)
    def _(i):
        follow = jnp.minimum(i + 1, nx - 1)
        inside = jnp.where(i < nx - 1, 1.0, 0.0).astype(F32)
        for f in range(2):
            own = conduct[f, at(i)]
            ahead = harmonic(own, conduct[f, at(follow)]) * inside
            wx[f, at(i + 1)] = ahead
            y_hi = jnp.where(row < ny - 1, harmonic(own, pltpu.roll(own, ny - 1, 0)), 0.0)
            y_lo = pltpu.roll(y_hi, 1, 0)
            z_hi = jnp.where(lane < nz - 1, harmonic(own, pltpu.roll(own, nz - 1, 1)), 0.0)
            z_lo = pltpu.roll(z_hi, 1, 1)
            wy[f, 0, at(i)] = y_lo
            wy[f, 1, at(i)] = y_hi
            wz[f, 0, at(i)] = z_lo
            wz[f, 1, at(i)] = z_hi
            total = capacity[f] + ahead + wx[f, at(i)] + y_lo + y_hi + z_lo + z_hi
            den[f, at(i)] = total
            inv[f, at(i)] = 1.0 / total

    levels = state + (final,)

    def sweep(step, start=0, stop=nx):
        @pl.loop(start, stop, unroll=16)
        def _(i):
            before = jnp.maximum(i - 1, 0)
            follow = jnp.minimum(i + 1, nx - 1)
            center = [state[step][f, at(i)] for f in range(2)]
            for f in range(2):
                c = center[f]
                acc = force[f, at(i)] + couple[f] * center[1 - f]
                acc = acc + wx[f, at(i)] * state[step][f, at(before)]
                acc = acc + wx[f, at(i + 1)] * state[step][f, at(follow)]
                acc = acc + wy[f, 0, at(i)] * pltpu.roll(c, 1, 0)
                acc = acc + wy[f, 1, at(i)] * pltpu.roll(c, ny - 1, 0)
                acc = acc + wz[f, 0, at(i)] * pltpu.roll(c, 1, 1)
                acc = acc + wz[f, 1, at(i)] * pltpu.roll(c, nz - 1, 1)
                levels[step + 1][f, at(i)] = acc * inv[f, at(i)]

    for side in range(2):
        wait_x(side, xrecv0.at[side], 0)

    for side in range(2):
        there = jnp.where(has_x[side], 1.0, 0.0).astype(F32)
        openness = open_of(xrecv0[side, 0:ny]) * there
        halo_conduct = (xrecv0[side, ny : 2 * ny] * openness, openness)
        for f in range(2):
            hwx[f, side] = harmonic(conduct[f, edge_plane[side]], halo_conduct[f])

    def ends(count, low, high):
        spot = lax.broadcasted_iota(jnp.int32, (count, nz), 0)
        return jnp.where(spot == 0, low, jnp.where(spot == count - 1, high, 0.0))

    sweep(0)

    for side in range(2):
        cut = edge_row[side]
        r = side * (ny - 1)
        own = [ysend0[side, (2 + f) * nx : (3 + f) * nx] for f in range(2)]
        for f in range(2):
            both = slice(f * nx, (f + 1) * nx)
            weight = [hwx[f, sx, r : r + 1] for sx in range(2)]
            flow = [
                weight[sx] * xrecv0[sx, (2 + f) * ny + r : (2 + f) * ny + r + 1] for sx in range(2)
            ]
            ysend[side, DEN, both] = den.at[f][cut, :] + ends(nx, *weight)
            ysend[side, OWN, both] = (
                force.at[f][cut, :]
                + couple[f] * own[1 - f]
                + wx.at[f][rows(r), :] * pltpu.roll(own[f], 1, 0)
                + wx.at[f][rows(r, 1), :] * pltpu.roll(own[f], nx - 1, 0)
                + wy.at[f, 1 - side][cut, :] * state[0].at[f][next_row[side], :]
                + wz.at[f, 0][cut, :] * pltpu.roll(own[f], 1, 1)
                + wz.at[f, 1][cut, :] * pltpu.roll(own[f], nz - 1, 1)
                + ends(nx, *flow)
            )
        send_y(OWN, 2, side)

    for side in range(2):
        cut = edge_plane[side]
        for f in range(2):
            w = hwx[f, side]
            old = den[f, cut]
            total = old + w
            inverse = 1.0 / total
            den[f, cut] = total
            inv[f, cut] = inverse
            value = xrecv0[side, (2 + f) * ny : (3 + f) * ny]
            state[1][f, cut] = (state[1][f, cut] * old + w * value) * inverse

    for side in range(2):
        wait_y(side, yrecv0.at[side, pl.ds(0, 2 * nx)], 0)
        wait_y(side, yrecv0.at[side, pl.ds(2 * nx, 2 * nx)], 1)

    for side in range(2):
        there = jnp.where(has_y[side], 1.0, 0.0).astype(F32)
        openness = open_of(yrecv0[side, 0:nx]) * there
        halo_conduct = (yrecv0[side, nx : 2 * nx] * openness, openness)
        cut = edge_row[side]
        for f in range(2):
            w = harmonic(conduct.at[f][cut, :], halo_conduct[f])
            hwy[f, side] = w
            old = den.at[f][cut, :]
            inverse = 1.0 / (old + w)
            inv.at[f][cut, :] = inverse
            known[side, f] = w * ysend0[side, (2 + f) * nx : (3 + f) * nx]
            value = yrecv0[side, (2 + f) * nx : (3 + f) * nx]
            state[1].at[f][cut, :] = (state[1].at[f][cut, :] * old + w * value) * inverse
    for side in range(2):
        send_x(ONE, side, [state[1].at[f, edge_plane[side]] for f in range(2)])

    sweep(1)

    for side in range(2):
        send_x(INV, side, [inv.at[f, edge_plane[side]] for f in range(2)])

    for side in range(2):
        for f in range(2):
            cut = edge_plane[side]
            scale = inv[f, cut]
            inner = wx[f, plane(1) if side == 0 else plane(nx - 1)]
            parts = (
                force[f, cut],
                couple[f],
                wy[f, 0, cut],
                wy[f, 1, cut],
                inner,
                wz[f, 0, cut],
                wz[f, 1, cut],
                hwx[f, side],
            )
            for n, part in enumerate(parts):
                xface[side, f, n] = part * scale
            xface[side, f, 8] = inner * inv[f, next_plane[side]]

            cut = edge_row[side]
            scale = inv.at[f][cut, :]
            inner = wy.at[f, 1 - side][cut, :]
            parts = (
                force.at[f][cut, :],
                couple[f],
                wx.at[f][rows(side * (ny - 1)), :],
                wx.at[f][rows(side * (ny - 1), 1), :],
                inner,
                wz.at[f, 0][cut, :],
                wz.at[f, 1][cut, :],
                hwy[f, side],
            )
            for n, part in enumerate(parts):
                yface[side, f, n] = part * scale
            yface[side, f, 8] = inner * inv.at[f][next_row[side], :]

    at_low = lane % TILE == 0
    at_high = lane % TILE == TILE - 1

    @pl.loop(0, nx, unroll=8)
    def _(i):
        d = damage[at(i + 1)]
        low = jnp.where(at_low & (lane > 0), pltpu.roll(d, 1, 1), 0.0)
        high = jnp.where(at_high & (lane < nz - 1), pltpu.roll(d, nz - 1, 1), 0.0)
        around[at(i)] = low + high

    for side in range(2):
        around[edge_plane[side], :] = around[edge_plane[side], :] + xrecv0[side, 0:ny]
    for side in range(2):
        around[edge_row[side], :] = around[edge_row[side], :] + yrecv0[side, 0:nx]
    arrived(tough, in_sem.at[2])
    arrived(roster, in_sem.at[3])
    tile_of = lane // TILE
    chosen = tile_of == roster[0]
    for n in range(1, roster.shape[0]):
        chosen = chosen | (tile_of == roster[n])
    listed[...] = jnp.where(chosen, 1.0, 0.0)

    def along(face, n, own):
        return (
            face[2] * pltpu.roll(own, 1, 0)
            + face[3] * pltpu.roll(own, n - 1, 0)
            + face[5] * pltpu.roll(own, 1, 1)
            + face[6] * pltpu.roll(own, nz - 1, 1)
        )

    for side in range(2):
        wait_x(side, xrecv.at[side, ONE], 1)
    for side in range(2):
        cut = edge_plane[side]
        for f in range(2):
            value = xrecv[side, ONE, f * ny : (f + 1) * ny]
            state[2][f, cut] = state[2][f, cut] + xface[side, f, 7] * value
    for side in range(2):
        wait_y(side, yrecv.at[side, pl.ds(OWN, 2)], 2)
        for f in range(2):
            cut = edge_row[side]
            both = slice(f * nx, (f + 1) * nx)
            inverse = 1.0 / (yrecv[side, DEN, both] + hwy[f, side])
            yinv[side, f] = inverse
            value = (yrecv[side, OWN, both] + known[side, f]) * inverse
            fresh = state[2].at[f][cut, :] + yface[side, f, 7] * value
            state[2].at[f][cut, :] = fresh
            ysend[side, Y_TWO, both] = fresh
        send_y(Y_TWO, 1, side)
        own = [ysend[side, Y_TWO, f * nx : (f + 1) * nx] for f in range(2)]
        for f in range(2):
            face = yface.at[side, f]
            inner = state[2].at[f][next_row[side], :]
            value = face[0] + face[1] * own[1 - f] + face[4] * inner + along(face, nx, own[f])
            ysend[side, Y_PART, f * nx : (f + 1) * nx] = value
        send_y(Y_PART, 1, side)
    for side in range(2):
        send_x(TWO, side, [state[2].at[f, edge_plane[side]] for f in range(2)])

    for c, (sx, sy) in enumerate(corners):
        xe = sx * (nx - 1)
        ye = sy * (ny - 1)
        for f in range(2):
            value = state[2][f, pl.ds(xe * ny + ye, 1), :]
            csend[c, f : f + 1] = hwx[f, sx, ye : ye + 1] * value
            csend[c, 2 + f : 3 + f] = hwy[f, sy, xe : xe + 1] * value

        @pl.when(has_c[c])
        def _():
            remote(csend.at[c], crecv.at[3 - c], send_sem.at[4 + c], cr.at[3 - c], to_c[c]).start()

    for side in range(2):
        own = [state[2][f, edge_plane[side]] for f in range(2)]
        for f in range(2):
            face = xface.at[side, f]
            inner = state[2][f, next_plane[side]]
            value = face[0] + face[1] * own[1 - f] + face[4] * inner + along(face, ny, own[f])
            xsend[side, f] = value
        send_x(PART, side, [xsend.at[side, f] for f in range(2)])

    sweep(2)
    sweep(3)

    for side in range(2):
        wait_x(side, xrecv.at[side, TWO], 2)
    for side in range(2):
        cut = edge_plane[side]
        cut_in = next_plane[side]
        change = [
            xface[side, f, 7] * xrecv[side, TWO, f * ny : (f + 1) * ny] for f in range(2)
        ]
        for f in range(2):
            face = xface.at[side, f]
            add = face[1] * change[1 - f] + along(face, ny, change[f])
            final[f, cut] = final[f, cut] + add
            final[f, cut_in] = final[f, cut_in] + face[8] * change[f]

    for side in range(2):
        wait_y(side, yrecv.at[side, Y_TWO], 3)
        cut = edge_row[side]
        cut_in = next_row[side]
        change = [
            yface[side, f, 7] * yrecv[side, Y_TWO, f * nx : (f + 1) * nx] for f in range(2)
        ]
        for f in range(2):
            face = yface.at[side, f]
            add = face[1] * change[1 - f] + along(face, nx, change[f])
            final.at[f][cut, :] = final.at[f][cut, :] + add
            final.at[f][cut_in, :] = final.at[f][cut_in, :] + face[8] * change[f]

    for side in range(2):
        wait_x(side, xrecv.at[side, pl.ds(PART, 2)], 3)
    for c in range(4):

        @pl.when(has_c[c])
        def _():
            arrived(crecv.at[c], cr.at[c])

    for side in range(2):
        cut = edge_plane[side]
        for f in range(2):
            both = slice(f * ny, (f + 1) * ny)
            more = ends(
                ny, crecv[2 * side, 2 + f : 3 + f], crecv[2 * side + 1, 2 + f : 3 + f]
            )
            beyond = xrecv[side, PART, both] + xrecv[side, INV, both] * (
                hwx[f, side] * state[2][f, cut] + more
            )
            final[f, cut] = final[f, cut] + xface[side, f, 7] * beyond

    for side in range(2):
        wait_y(side, yrecv.at[side, Y_PART], 4)
        cut = edge_row[side]
        for f in range(2):
            both = slice(f * nx, (f + 1) * nx)
            more = ends(nx, crecv[side, f : f + 1], crecv[2 + side, f : f + 1])
            more = more + hwy[f, side] * ysend[side, Y_TWO, both]
            beyond = yrecv[side, Y_PART, both] + yinv[side, f] * more
            final.at[f][cut, :] = final.at[f][cut, :] + yface[side, f, 7] * beyond

    for c in range(4):

        @pl.when(has_c[c])
        def _():
            arrived(csend.at[c], send_sem.at[4 + c])

    for side in range(2):

        @pl.when(has_y[side])
        def _():
            arrived(fixed.at[0, pl.ds(0, (4 + 2 * SENDS) * nx)], send_sem.at[2 + side])

        @pl.when(has_x[side])
        def _():
            arrived(fixed.at[0, pl.ds(0, (4 + 2 * SENDS) * ny)], send_sem.at[side])


def finish(
    sizes,
    final,
    damage,
    around,
    tough,
    listed,
    p_out,
    t_out,
    d_out,
    work0,
    work1,
    da,
    db,
    out_sem,
):
    nx, ny, nz = sizes
    cells = nx * ny
    row = lax.broadcasted_iota(jnp.int32, (ny, nz), 0)
    lane = lax.broadcasted_iota(jnp.int32, (ny, nz), 1)

    def at(i):
        return pl.ds(pl.multiple_of(i * ny, ny), ny)

    outs = [
        pltpu.make_async_copy(final.at[0], p_out, out_sem.at[0]),
        pltpu.make_async_copy(final.at[1], t_out, out_sem.at[0]),
    ]
    for out in outs:
        out.start()

    zero_plane = jnp.zeros((ny, nz), F32)
    for work in (work0, work1):
        work[0:ny] = zero_plane
        work[(nx + 1) * ny : (nx + 2) * ny] = zero_plane

    y_first = row == 0
    y_last = row == ny - 1
    z_first = lane % TILE == 0
    z_last = lane % TILE == TILE - 1
    inside = listed[...] > 0.0

    piece = cells // CHUNKS
    last = [
        pltpu.make_async_copy(
            work0.at[pl.ds(ny + chunk * piece, piece)],
            d_out.at[pl.ds(chunk * piece, piece)],
            out_sem.at[1],
        )
        for chunk in range(CHUNKS)
    ]
    for step in range(DAMAGE_SWEEPS):
        source = (damage, work0, work1)[step % 3]
        target = (work0, work1, work0)[step % 3]

        def relax(i):
            d = source[at(i + 1)]
            near = around[at(i)] + source[at(i)] + source[at(i + 2)]
            near = near + jnp.where(y_first, 0.0, pltpu.roll(d, 1, 0))
            near = near + jnp.where(y_last, 0.0, pltpu.roll(d, ny - 1, 0))
            near = near + jnp.where(z_first, 0.0, pltpu.roll(d, 1, 1))
            near = near + jnp.where(z_last, 0.0, pltpu.roll(d, nz - 1, 1))
            if step == 0:
                load = final[0, at(i)]
                hard = tough[at(i)]
                drive = 2.0 * energy_scale * load * load
                spread = hard * crack_length
                inverse = 1.0 / (hard / crack_length + drive + 6.0 * spread)
                a = drive * inverse
                b = spread * inverse
                da[at(i)] = a
                db[at(i)] = b
            else:
                a = da[at(i)]
                b = db[at(i)]
            fresh = a + b * near
            if step == DAMAGE_SWEEPS - 1:
                fresh = jnp.where(inside, fresh, damage[at(i + 1)])
            target[at(i + 1)] = fresh

        if step < DAMAGE_SWEEPS - 1:
            pl.loop(0, nx, unroll=nx)(relax)
        else:
            for chunk in range(CHUNKS):
                pl.loop(chunk * nx // CHUNKS, (chunk + 1) * nx // CHUNKS, unroll=nx // CHUNKS)(relax)
                last[chunk].start()

    pltpu.make_async_copy(final, final, out_sem.at[0]).wait()
    whole = work0.at[pl.ds(ny, cells)]
    pltpu.make_async_copy(whole, whole, out_sem.at[1]).wait()


def body(counts, names, *arrays):
    nx, ny, nz = arrays[0].shape
    cells = nx * ny
    flat = [a.reshape(cells, nz) for a in arrays[:-1]] + [arrays[-1]]
    flat = [pltpu.with_memory_space_constraint(a, pltpu.HBM) for a in flat]
    block = jax.ShapeDtypeStruct((cells, nz), F32)
    dma = pltpu.SemaphoreType.DMA
    vmem = pl.BlockSpec(memory_space=pltpu.VMEM)
    hbm = pl.BlockSpec(memory_space=pl.ANY)
    middle = pl.pallas_call(
        functools.partial(kernel, names, (nx, ny, nz) + counts),
        out_shape=(
            jax.ShapeDtypeStruct((2, cells, nz), F32),
            jax.ShapeDtypeStruct((cells + 2 * ny, nz), F32),
            block,
            block,
            jax.ShapeDtypeStruct((ny, nz), F32),
        ),
        in_specs=[hbm] * 8,
        out_specs=[vmem] * 5,
        scratch_shapes=[
            pltpu.VMEM((2, cells, nz), F32),
            pltpu.VMEM((2, cells, nz), F32),
            pltpu.VMEM((2, cells, nz), F32),
            pltpu.VMEM((2, cells, nz), F32),
            pltpu.VMEM((3, cells, nz), F32),
            pltpu.VMEM((2, cells, nz), F32),
            pltpu.VMEM((2, cells, nz), F32),
            pltpu.VMEM((2, cells + ny, nz), F32),
            pltpu.VMEM((2, 2, cells, nz), F32),
            pltpu.VMEM((2, 2, cells, nz), F32),
            pltpu.VMEM((2, cells, nz), F32),
            pltpu.VMEM((2, cells, nz), F32),
            pltpu.VMEM((2, 2, ny, nz), F32),
            pltpu.VMEM((2, 2, nx, nz), F32),
            pltpu.VMEM((2, 2, 9, ny, nz), F32),
            pltpu.VMEM((2, 2, 9, nx, nz), F32),
            pltpu.VMEM((2, 4 * nx, nz), F32),
            pltpu.VMEM((2, 4 * nx, nz), F32),
            pltpu.VMEM((2, 4 * ny, nz), F32),
            pltpu.VMEM((2, SENDS, 2 * nx, nz), F32),
            pltpu.VMEM((2, SENDS, 2 * nx, nz), F32),
            pltpu.VMEM((2, 2, ny, nz), F32),
            pltpu.VMEM((2, SENDS, 2 * ny, nz), F32),
            pltpu.VMEM((4, 8, nz), F32),
            pltpu.VMEM((4, 8, nz), F32),
            pltpu.VMEM((2, 2, nx, nz), F32),
            pltpu.VMEM((2, 2, nx, nz), F32),
            pltpu.SMEM(arrays[-1].shape, jnp.int32),
            dma((4,)),
            dma((8,)),
            dma((2, 4)),
            dma((2, 5)),
            dma((4,)),
        ],
        compiler_params=pltpu.CompilerParams(
            collective_id=0, has_side_effects=True, vmem_limit_bytes=40 * 2**20
        ),
    )(*flat)
    outs = pl.pallas_call(
        functools.partial(finish, (nx, ny, nz)),
        out_shape=(block, block, block),
        in_specs=[vmem] * 5,
        out_specs=[hbm] * 3,
        scratch_shapes=[
            pltpu.VMEM((cells + 2 * ny, nz), F32),
            pltpu.VMEM((cells + 2 * ny, nz), F32),
            pltpu.VMEM((cells, nz), F32),
            pltpu.VMEM((cells, nz), F32),
            dma((2,)),
        ],
        compiler_params=pltpu.CompilerParams(vmem_limit_bytes=16 * 2**20),
    )(*middle)
    return tuple(o.reshape(nx, ny, nz) for o in outs)


def solution(mesh):
    cut = P("gx", "gy", None)
    names = ("gx", "gy")
    counts = (mesh.shape["gx"], mesh.shape["gy"])
    return jax.shard_map(
        functools.partial(body, counts, names),
        mesh=mesh,
        in_specs=(cut,) * 7 + (P(("gx", "gy")),),
        out_specs=(cut, cut, cut),
        check_vma=False,
    )
```

```python
import functools

import jax
import jax.numpy as jnp
from jax import lax
from jax.experimental import pallas as pl
from jax.experimental.pallas import tpu as pltpu
from jax.sharding import PartitionSpec as P

TILE = 32
SWEEPS = 4
DAMAGE_SWEEPS = 3
CHUNKS = 4
ONE, TWO, PART, INV = range(4)
OWN, DEN, Y_TWO, Y_PART = range(4)
SENDS = 4

capacity = (0.5, 0.5)
couple = (0.3, 0.3)
residual_open = 0.05
harmonic_floor = 0.001
crack_length = 2.0
energy_scale = 2.0
F32 = jnp.float32


def harmonic(left, right):
    return 2.0 * left * right / (left + right + harmonic_floor)


def kernel(
    names,
    sizes,
    p_hbm,
    t_hbm,
    d_hbm,
    k_hbm,
    g_hbm,
    qp_hbm,
    qt_hbm,
    roster_hbm,
    final,
    damage,
    around,
    begin,
    tough,
    listed,
    state0,
    state1,
    state2,
    state3,
    fixed,
    force,
    conduct,
    wx,
    wy,
    wz,
    den,
    inv,
    hwx,
    hwy,
    xface,
    yface,
    ysend0,
    yrecv0,
    xrecv0,
    ysend,
    yrecv,
    xsend,
    xrecv,
    csend,
    crecv,
    known,
    yinv,
    roster,
    in_sem,
    send_sem,
    xr,
    yr,
    cr,
):
    nx, ny, nz, count_x, count_y = sizes
    cells = nx * ny
    state = (state0, state1, state2, state3)
    gx, gy = names
    ix = lax.axis_index(gx)
    iy = lax.axis_index(gy)
    has_x = (ix > 0, ix < count_x - 1)
    has_y = (iy > 0, iy < count_y - 1)
    to_x = ({gx: ix - 1}, {gx: ix + 1})
    to_y = ({gy: iy - 1}, {gy: iy + 1})
    corners = [(sx, sy) for sx in range(2) for sy in range(2)]
    has_c = [has_x[sx] & has_y[sy] for sx, sy in corners]
    to_c = [to_x[sx] | to_y[sy] for sx, sy in corners]
    mesh_type = pl.DeviceIdType.MESH

    barrier = pltpu.get_barrier_semaphore()
    for has, to in ((has_y, to_y), (has_x, to_x)):
        for side in range(2):

            @pl.when(has[side])
            def _():
                pl.semaphore_signal(barrier, inc=1, device_id=to[side], device_id_type=mesh_type)

    load = pltpu.make_async_copy
    first = [
        load(d_hbm, damage.at[pl.ds(ny, cells)], in_sem.at[0]),
        load(k_hbm, fixed.at[0], in_sem.at[0]),
        load(p_hbm, state[0].at[0], in_sem.at[0]),
        load(t_hbm, state[0].at[1], in_sem.at[0]),
    ]
    rates = [
        load(qp_hbm, fixed.at[1], in_sem.at[1]),
        load(qt_hbm, fixed.at[2], in_sem.at[1]),
    ]
    late = [
        load(g_hbm, tough, in_sem.at[2]),
        load(roster_hbm, roster, in_sem.at[3]),
    ]
    for copy in first + rates + late:
        copy.start()

    def arrived(ref, sem):
        pltpu.make_async_copy(ref, ref, sem).wait()

    csend[...] = jnp.zeros(csend.shape, F32)
    for c in range(4):

        @pl.when(jnp.logical_not(has_c[c]))
        def _():
            crecv[c] = jnp.zeros(crecv.shape[1:], F32)

    for side in range(2):

        @pl.when(jnp.logical_not(has_x[side]))
        def _():
            xrecv0[side] = jnp.zeros(xrecv0.shape[1:], F32)
            for step in range(SENDS):
                xrecv[side, step] = jnp.zeros(xrecv.shape[2:], F32)

        @pl.when(jnp.logical_not(has_y[side]))
        def _():
            yrecv0[side] = jnp.zeros(yrecv0.shape[1:], F32)
            for step in range(SENDS):
                yrecv[side, step] = jnp.full(yrecv.shape[2:], float(step == DEN), F32)

    zero_plane = jnp.zeros((ny, nz), F32)
    damage[0:ny] = zero_plane
    damage[(nx + 1) * ny : (nx + 2) * ny] = zero_plane
    for f in range(2):
        wx[f, 0:ny] = zero_plane
        wx[f, nx * ny : (nx + 1) * ny] = zero_plane

    def rows(r, first_plane=0):
        return pl.ds(first_plane * ny + r, nx, stride=ny)

    def plane(i):
        return pl.ds(i * ny, ny)

    edge_row = (rows(0), rows(ny - 1))
    next_row = (rows(1), rows(ny - 2))
    edge_plane = (plane(0), plane(nx - 1))
    next_plane = (plane(1), plane(nx - 2))
    edge_pad = (rows(0, 1), rows(ny - 1, 1))
    edge_plane_pad = (plane(1), plane(nx))

    arrived(wy, in_sem.at[0])

    for side in range(2):
        ysend0[side, 0 * nx : 1 * nx] = damage[edge_pad[side], :]
        ysend0[side, 1 * nx : 2 * nx] = fixed.at[0][edge_row[side], :]
        ysend0[side, 2 * nx : 3 * nx] = state[0].at[0][edge_row[side], :]
        ysend0[side, 3 * nx : 4 * nx] = state[0].at[1][edge_row[side], :]

    def remote(source, target, send, recv, to):
        return pltpu.make_async_remote_copy(
            src_ref=source,
            dst_ref=target,
            send_sem=send,
            recv_sem=recv,
            device_id=to,
            device_id_type=mesh_type,
        )

    place = {ONE: 1, TWO: 2, PART: 3, INV: 3}

    def send_y(step, count, side):
        @pl.when(has_y[side])
        def _():
            remote(
                ysend.at[side, pl.ds(step, count)],
                yrecv.at[1 - side, pl.ds(step, count)],
                send_sem.at[2 + side],
                yr.at[1 - side, {OWN: 2, Y_TWO: 3, Y_PART: 4}[step]],
                to_y[side],
            ).start()

    def send_x(step, side, sources):
        @pl.when(has_x[side])
        def _():
            for f in range(2):
                remote(
                    sources[f],
                    xrecv.at[1 - side, step, pl.ds(f * ny, ny)],
                    send_sem.at[side],
                    xr.at[1 - side, place[step]],
                    to_x[side],
                ).start()

    def wait_y(side, ref, n):
        @pl.when(has_y[side])
        def _():
            arrived(ref, yr.at[side, n])

    def wait_x(side, ref, n):
        @pl.when(has_x[side])
        def _():
            arrived(ref, xr.at[side, n])

    peers = sum(jnp.where(has, 1, 0).astype(jnp.int32) for has in has_x + has_y)
    pl.semaphore_wait(barrier, peers)

    for half in range(2):
        for side in range(2):

            @pl.when(has_y[side])
            def _():
                part = pl.ds(half * 2 * nx, 2 * nx)
                remote(
                    ysend0.at[side, part],
                    yrecv0.at[1 - side, part],
                    send_sem.at[2 + side],
                    yr.at[1 - side, half],
                    to_y[side],
                ).start()

    for side in range(2):
        sources = (
            damage.at[edge_plane_pad[side]],
            fixed.at[0, edge_plane[side]],
            state[0].at[0, edge_plane[side]],
            state[0].at[1, edge_plane[side]],
        )

        @pl.when(has_x[side])
        def _():
            for n, source in enumerate(sources):
                remote(
                    source,
                    xrecv0.at[1 - side, pl.ds(n * ny, ny)],
                    send_sem.at[side],
                    xr.at[1 - side, 0],
                    to_x[side],
                ).start()

    row = lax.broadcasted_iota(jnp.int32, (ny, nz), 0)
    lane = lax.broadcasted_iota(jnp.int32, (ny, nz), 1)

    def at(i):
        return pl.ds(pl.multiple_of(i * ny, ny), ny)

    def open_of(d):
        return (1.0 - d) * (1.0 - d) + residual_open

    arrived(fixed.at[pl.ds(1, 2)], in_sem.at[1])

    @pl.loop(0, nx, unroll=8)
    def _(i):
        openness = open_of(damage[at(i + 1)])
        conduct[1, at(i)] = openness
        conduct[0, at(i)] = fixed[0, at(i)] * openness
        for f in range(2):
            force[f, at(i)] = fixed[1 + f, at(i)] + capacity[f] * state[0][f, at(i)]

    @pl.loop(0, nx, unroll=8)
    def _(i):
        follow = jnp.minimum(i + 1, nx - 1)
        inside = jnp.where(i < nx - 1, 1.0, 0.0).astype(F32)
        for f in range(2):
            own = conduct[f, at(i)]
            ahead = harmonic(own, conduct[f, at(follow)]) * inside
            wx[f, at(i + 1)] = ahead
            y_hi = jnp.where(row < ny - 1, harmonic(own, pltpu.roll(own, ny - 1, 0)), 0.0)
            y_lo = pltpu.roll(y_hi, 1, 0)
            z_hi = jnp.where(lane < nz - 1, harmonic(own, pltpu.roll(own, nz - 1, 1)), 0.0)
            z_lo = pltpu.roll(z_hi, 1, 1)
            wy[f, 0, at(i)] = y_lo
            wy[f, 1, at(i)] = y_hi
            wz[f, 0, at(i)] = z_lo
            wz[f, 1, at(i)] = z_hi
            total = capacity[f] + ahead + wx[f, at(i)] + y_lo + y_hi + z_lo + z_hi
            den[f, at(i)] = total
            inv[f, at(i)] = 1.0 / total

    levels = state + (final,)

    def sweep(step, start=0, stop=nx):
        @pl.loop(start, stop, unroll=16)
        def _(i):
            before = jnp.maximum(i - 1, 0)
            follow = jnp.minimum(i + 1, nx - 1)
            center = [state[step][f, at(i)] for f in range(2)]
            for f in range(2):
                c = center[f]
                acc = force[f, at(i)] + couple[f] * center[1 - f]
                acc = acc + wx[f, at(i)] * state[step][f, at(before)]
                acc = acc + wx[f, at(i + 1)] * state[step][f, at(follow)]
                acc = acc + wy[f, 0, at(i)] * pltpu.roll(c, 1, 0)
                acc = acc + wy[f, 1, at(i)] * pltpu.roll(c, ny - 1, 0)
                acc = acc + wz[f, 0, at(i)] * pltpu.roll(c, 1, 1)
                acc = acc + wz[f, 1, at(i)] * pltpu.roll(c, nz - 1, 1)
                levels[step + 1][f, at(i)] = acc * inv[f, at(i)]

    for side in range(2):
        wait_x(side, xrecv0.at[side], 0)

    for side in range(2):
        there = jnp.where(has_x[side], 1.0, 0.0).astype(F32)
        openness = open_of(xrecv0[side, 0:ny]) * there
        halo_conduct = (xrecv0[side, ny : 2 * ny] * openness, openness)
        for f in range(2):
            hwx[f, side] = harmonic(conduct[f, edge_plane[side]], halo_conduct[f])

    def ends(count, low, high):
        spot = lax.broadcasted_iota(jnp.int32, (count, nz), 0)
        return jnp.where(spot == 0, low, jnp.where(spot == count - 1, high, 0.0))

    sweep(0)

    for side in range(2):
        cut = edge_row[side]
        r = side * (ny - 1)
        own = [ysend0[side, (2 + f) * nx : (3 + f) * nx] for f in range(2)]
        for f in range(2):
            both = slice(f * nx, (f + 1) * nx)
            weight = [hwx[f, sx, r : r + 1] for sx in range(2)]
            flow = [
                weight[sx] * xrecv0[sx, (2 + f) * ny + r : (2 + f) * ny + r + 1] for sx in range(2)
            ]
            ysend[side, DEN, both] = den.at[f][cut, :] + ends(nx, *weight)
            ysend[side, OWN, both] = (
                force.at[f][cut, :]
                + couple[f] * own[1 - f]
                + wx.at[f][rows(r), :] * pltpu.roll(own[f], 1, 0)
                + wx.at[f][rows(r, 1), :] * pltpu.roll(own[f], nx - 1, 0)
                + wy.at[f, 1 - side][cut, :] * state[0].at[f][next_row[side], :]
                + wz.at[f, 0][cut, :] * pltpu.roll(own[f], 1, 1)
                + wz.at[f, 1][cut, :] * pltpu.roll(own[f], nz - 1, 1)
                + ends(nx, *flow)
            )
        send_y(OWN, 2, side)

    for side in range(2):
        cut = edge_plane[side]
        for f in range(2):
            w = hwx[f, side]
            old = den[f, cut]
            total = old + w
            inverse = 1.0 / total
            den[f, cut] = total
            inv[f, cut] = inverse
            value = xrecv0[side, (2 + f) * ny : (3 + f) * ny]
            state[1][f, cut] = (state[1][f, cut] * old + w * value) * inverse

    for side in range(2):
        wait_y(side, yrecv0.at[side, pl.ds(0, 2 * nx)], 0)
        wait_y(side, yrecv0.at[side, pl.ds(2 * nx, 2 * nx)], 1)

    for side in range(2):
        there = jnp.where(has_y[side], 1.0, 0.0).astype(F32)
        openness = open_of(yrecv0[side, 0:nx]) * there
        halo_conduct = (yrecv0[side, nx : 2 * nx] * openness, openness)
        cut = edge_row[side]
        for f in range(2):
            w = harmonic(conduct.at[f][cut, :], halo_conduct[f])
            hwy[f, side] = w
            old = den.at[f][cut, :]
            inverse = 1.0 / (old + w)
            inv.at[f][cut, :] = inverse
            known[side, f] = w * ysend0[side, (2 + f) * nx : (3 + f) * nx]
            value = yrecv0[side, (2 + f) * nx : (3 + f) * nx]
            state[1].at[f][cut, :] = (state[1].at[f][cut, :] * old + w * value) * inverse
    for side in range(2):
        send_x(ONE, side, [state[1].at[f, edge_plane[side]] for f in range(2)])

    sweep(1)

    for side in range(2):
        send_x(INV, side, [inv.at[f, edge_plane[side]] for f in range(2)])

    for side in range(2):
        for f in range(2):
            cut = edge_plane[side]
            scale = inv[f, cut]
            inner = wx[f, plane(1) if side == 0 else plane(nx - 1)]
            parts = (
                force[f, cut],
                couple[f],
                wy[f, 0, cut],
                wy[f, 1, cut],
                inner,
                wz[f, 0, cut],
                wz[f, 1, cut],
                hwx[f, side],
            )
            for n, part in enumerate(parts):
                xface[side, f, n] = part * scale
            xface[side, f, 8] = inner * inv[f, next_plane[side]]

            cut = edge_row[side]
            scale = inv.at[f][cut, :]
            inner = wy.at[f, 1 - side][cut, :]
            parts = (
                force.at[f][cut, :],
                couple[f],
                wx.at[f][rows(side * (ny - 1)), :],
                wx.at[f][rows(side * (ny - 1), 1), :],
                inner,
                wz.at[f, 0][cut, :],
                wz.at[f, 1][cut, :],
                hwy[f, side],
            )
            for n, part in enumerate(parts):
                yface[side, f, n] = part * scale
            yface[side, f, 8] = inner * inv.at[f][next_row[side], :]

    def along(face, n, own):
        return (
            face[2] * pltpu.roll(own, 1, 0)
            + face[3] * pltpu.roll(own, n - 1, 0)
            + face[5] * pltpu.roll(own, 1, 1)
            + face[6] * pltpu.roll(own, nz - 1, 1)
        )

    for side in range(2):
        wait_x(side, xrecv.at[side, ONE], 1)
    for side in range(2):
        cut = edge_plane[side]
        for f in range(2):
            value = xrecv[side, ONE, f * ny : (f + 1) * ny]
            state[2][f, cut] = state[2][f, cut] + xface[side, f, 7] * value
    for side in range(2):
        wait_y(side, yrecv.at[side, pl.ds(OWN, 2)], 2)
        for f in range(2):
            cut = edge_row[side]
            both = slice(f * nx, (f + 1) * nx)
            inverse = 1.0 / (yrecv[side, DEN, both] + hwy[f, side])
            yinv[side, f] = inverse
            value = (yrecv[side, OWN, both] + known[side, f]) * inverse
            fresh = state[2].at[f][cut, :] + yface[side, f, 7] * value
            state[2].at[f][cut, :] = fresh
            ysend[side, Y_TWO, both] = fresh
        send_y(Y_TWO, 1, side)
        own = [ysend[side, Y_TWO, f * nx : (f + 1) * nx] for f in range(2)]
        for f in range(2):
            face = yface.at[side, f]
            inner = state[2].at[f][next_row[side], :]
            value = face[0] + face[1] * own[1 - f] + face[4] * inner + along(face, nx, own[f])
            ysend[side, Y_PART, f * nx : (f + 1) * nx] = value
        send_y(Y_PART, 1, side)
    for side in range(2):
        send_x(TWO, side, [state[2].at[f, edge_plane[side]] for f in range(2)])

    for c, (sx, sy) in enumerate(corners):
        xe = sx * (nx - 1)
        ye = sy * (ny - 1)
        for f in range(2):
            value = state[2][f, pl.ds(xe * ny + ye, 1), :]
            csend[c, f : f + 1] = hwx[f, sx, ye : ye + 1] * value
            csend[c, 2 + f : 3 + f] = hwy[f, sy, xe : xe + 1] * value

        @pl.when(has_c[c])
        def _():
            remote(csend.at[c], crecv.at[3 - c], send_sem.at[4 + c], cr.at[3 - c], to_c[c]).start()

    for side in range(2):
        own = [state[2][f, edge_plane[side]] for f in range(2)]
        for f in range(2):
            face = xface.at[side, f]
            inner = state[2][f, next_plane[side]]
            value = face[0] + face[1] * own[1 - f] + face[4] * inner + along(face, ny, own[f])
            xsend[side, f] = value
        send_x(PART, side, [xsend.at[side, f] for f in range(2)])

    sweep(2)
    sweep(3)

    at_low = lane % TILE == 0
    at_high = lane % TILE == TILE - 1

    @pl.loop(0, nx, unroll=8)
    def _(i):
        d = damage[at(i + 1)]
        low = jnp.where(at_low & (lane > 0), pltpu.roll(d, 1, 1), 0.0)
        high = jnp.where(at_high & (lane < nz - 1), pltpu.roll(d, nz - 1, 1), 0.0)
        around[at(i)] = low + high

    for side in range(2):
        around[edge_plane[side], :] = around[edge_plane[side], :] + xrecv0[side, 0:ny]
    for side in range(2):
        around[edge_row[side], :] = around[edge_row[side], :] + yrecv0[side, 0:nx]
    arrived(tough, in_sem.at[2])
    arrived(roster, in_sem.at[3])
    tile_of = lane // TILE
    chosen = tile_of == roster[0]
    for n in range(1, roster.shape[0]):
        chosen = chosen | (tile_of == roster[n])
    listed[...] = jnp.where(chosen, 1.0, 0.0)

    @pl.loop(0, nx, unroll=8)
    def _(i):
        d = damage[at(i + 1)]
        near = around[at(i)] + damage[at(i)] + damage[at(i + 2)]
        near = near + jnp.where(row == 0, 0.0, pltpu.roll(d, 1, 0))
        near = near + jnp.where(row == ny - 1, 0.0, pltpu.roll(d, ny - 1, 0))
        near = near + jnp.where(at_low, 0.0, pltpu.roll(d, 1, 1))
        near = near + jnp.where(at_high, 0.0, pltpu.roll(d, nz - 1, 1))
        begin[at(i)] = near

    for side in range(2):
        wait_x(side, xrecv.at[side, TWO], 2)
    for side in range(2):
        cut = edge_plane[side]
        cut_in = next_plane[side]
        change = [
            xface[side, f, 7] * xrecv[side, TWO, f * ny : (f + 1) * ny] for f in range(2)
        ]
        for f in range(2):
            face = xface.at[side, f]
            add = face[1] * change[1 - f] + along(face, ny, change[f])
            final[f, cut] = final[f, cut] + add
            final[f, cut_in] = final[f, cut_in] + face[8] * change[f]

    for side in range(2):
        wait_y(side, yrecv.at[side, Y_TWO], 3)
        cut = edge_row[side]
        cut_in = next_row[side]
        change = [
            yface[side, f, 7] * yrecv[side, Y_TWO, f * nx : (f + 1) * nx] for f in range(2)
        ]
        for f in range(2):
            face = yface.at[side, f]
            add = face[1] * change[1 - f] + along(face, nx, change[f])
            final.at[f][cut, :] = final.at[f][cut, :] + add
            final.at[f][cut_in, :] = final.at[f][cut_in, :] + face[8] * change[f]

    for side in range(2):
        wait_x(side, xrecv.at[side, pl.ds(PART, 2)], 3)
    for c in range(4):

        @pl.when(has_c[c])
        def _():
            arrived(crecv.at[c], cr.at[c])

    for side in range(2):
        cut = edge_plane[side]
        for f in range(2):
            both = slice(f * ny, (f + 1) * ny)
            more = ends(
                ny, crecv[2 * side, 2 + f : 3 + f], crecv[2 * side + 1, 2 + f : 3 + f]
            )
            beyond = xrecv[side, PART, both] + xrecv[side, INV, both] * (
                hwx[f, side] * state[2][f, cut] + more
            )
            final[f, cut] = final[f, cut] + xface[side, f, 7] * beyond

    for side in range(2):
        wait_y(side, yrecv.at[side, Y_PART], 4)
        cut = edge_row[side]
        for f in range(2):
            both = slice(f * nx, (f + 1) * nx)
            more = ends(nx, crecv[side, f : f + 1], crecv[2 + side, f : f + 1])
            more = more + hwy[f, side] * ysend[side, Y_TWO, both]
            beyond = yrecv[side, Y_PART, both] + yinv[side, f] * more
            final.at[f][cut, :] = final.at[f][cut, :] + yface[side, f, 7] * beyond

    for c in range(4):

        @pl.when(has_c[c])
        def _():
            arrived(csend.at[c], send_sem.at[4 + c])

    for side in range(2):

        @pl.when(has_y[side])
        def _():
            arrived(fixed.at[0, pl.ds(0, (4 + 2 * SENDS) * nx)], send_sem.at[2 + side])

        @pl.when(has_x[side])
        def _():
            arrived(fixed.at[0, pl.ds(0, (4 + 2 * SENDS) * ny)], send_sem.at[side])


def finish(
    sizes,
    final,
    damage,
    around,
    begin,
    tough,
    listed,
    p_out,
    t_out,
    d_out,
    work0,
    work1,
    da,
    db,
    out_sem,
):
    nx, ny, nz = sizes
    cells = nx * ny
    row = lax.broadcasted_iota(jnp.int32, (ny, nz), 0)
    lane = lax.broadcasted_iota(jnp.int32, (ny, nz), 1)

    def at(i):
        return pl.ds(pl.multiple_of(i * ny, ny), ny)

    outs = [
        pltpu.make_async_copy(final.at[0], p_out, out_sem.at[0]),
        pltpu.make_async_copy(final.at[1], t_out, out_sem.at[0]),
    ]
    for out in outs:
        out.start()

    zero_plane = jnp.zeros((ny, nz), F32)
    for work in (work0, work1):
        work[0:ny] = zero_plane
        work[(nx + 1) * ny : (nx + 2) * ny] = zero_plane

    y_first = row == 0
    y_last = row == ny - 1
    z_first = lane % TILE == 0
    z_last = lane % TILE == TILE - 1
    inside = listed[...] > 0.0

    piece = cells // CHUNKS
    last = [
        pltpu.make_async_copy(
            work0.at[pl.ds(ny + chunk * piece, piece)],
            d_out.at[pl.ds(chunk * piece, piece)],
            out_sem.at[1],
        )
        for chunk in range(CHUNKS)
    ]
    for step in range(DAMAGE_SWEEPS):
        source = (damage, work0, work1)[step % 3]
        target = (work0, work1, work0)[step % 3]

        def relax(i):
            d = source[at(i + 1)]
            if step == 0:
                near = begin[at(i)]
            else:
                near = around[at(i)] + source[at(i)] + source[at(i + 2)]
                near = near + jnp.where(y_first, 0.0, pltpu.roll(d, 1, 0))
                near = near + jnp.where(y_last, 0.0, pltpu.roll(d, ny - 1, 0))
                near = near + jnp.where(z_first, 0.0, pltpu.roll(d, 1, 1))
                near = near + jnp.where(z_last, 0.0, pltpu.roll(d, nz - 1, 1))
            if step == 0:
                load = final[0, at(i)]
                hard = tough[at(i)]
                drive = 2.0 * energy_scale * load * load
                spread = hard * crack_length
                inverse = 1.0 / (hard / crack_length + drive + 6.0 * spread)
                a = drive * inverse
                b = spread * inverse
                da[at(i)] = a
                db[at(i)] = b
            else:
                a = da[at(i)]
                b = db[at(i)]
            fresh = a + b * near
            if step == DAMAGE_SWEEPS - 1:
                fresh = jnp.where(inside, fresh, damage[at(i + 1)])
            target[at(i + 1)] = fresh

        if step < DAMAGE_SWEEPS - 1:
            pl.loop(0, nx, unroll=nx)(relax)
        else:
            for chunk in range(CHUNKS):
                pl.loop(chunk * nx // CHUNKS, (chunk + 1) * nx // CHUNKS, unroll=nx // CHUNKS)(relax)
                last[chunk].start()

    pltpu.make_async_copy(final, final, out_sem.at[0]).wait()
    whole = work0.at[pl.ds(ny, cells)]
    pltpu.make_async_copy(whole, whole, out_sem.at[1]).wait()


def body(counts, names, *arrays):
    nx, ny, nz = arrays[0].shape
    cells = nx * ny
    flat = [a.reshape(cells, nz) for a in arrays[:-1]] + [arrays[-1]]
    flat = [pltpu.with_memory_space_constraint(a, pltpu.HBM) for a in flat]
    block = jax.ShapeDtypeStruct((cells, nz), F32)
    dma = pltpu.SemaphoreType.DMA
    vmem = pl.BlockSpec(memory_space=pltpu.VMEM)
    hbm = pl.BlockSpec(memory_space=pl.ANY)
    middle = pl.pallas_call(
        functools.partial(kernel, names, (nx, ny, nz) + counts),
        out_shape=(
            jax.ShapeDtypeStruct((2, cells, nz), F32),
            jax.ShapeDtypeStruct((cells + 2 * ny, nz), F32),
            block,
            block,
            block,
            jax.ShapeDtypeStruct((ny, nz), F32),
        ),
        in_specs=[hbm] * 8,
        out_specs=[vmem] * 6,
        scratch_shapes=[
            pltpu.VMEM((2, cells, nz), F32),
            pltpu.VMEM((2, cells, nz), F32),
            pltpu.VMEM((2, cells, nz), F32),
            pltpu.VMEM((2, cells, nz), F32),
            pltpu.VMEM((3, cells, nz), F32),
            pltpu.VMEM((2, cells, nz), F32),
            pltpu.VMEM((2, cells, nz), F32),
            pltpu.VMEM((2, cells + ny, nz), F32),
            pltpu.VMEM((2, 2, cells, nz), F32),
            pltpu.VMEM((2, 2, cells, nz), F32),
            pltpu.VMEM((2, cells, nz), F32),
            pltpu.VMEM((2, cells, nz), F32),
            pltpu.VMEM((2, 2, ny, nz), F32),
            pltpu.VMEM((2, 2, nx, nz), F32),
            pltpu.VMEM((2, 2, 9, ny, nz), F32),
            pltpu.VMEM((2, 2, 9, nx, nz), F32),
            pltpu.VMEM((2, 4 * nx, nz), F32),
            pltpu.VMEM((2, 4 * nx, nz), F32),
            pltpu.VMEM((2, 4 * ny, nz), F32),
            pltpu.VMEM((2, SENDS, 2 * nx, nz), F32),
            pltpu.VMEM((2, SENDS, 2 * nx, nz), F32),
            pltpu.VMEM((2, 2, ny, nz), F32),
            pltpu.VMEM((2, SENDS, 2 * ny, nz), F32),
            pltpu.VMEM((4, 8, nz), F32),
            pltpu.VMEM((4, 8, nz), F32),
            pltpu.VMEM((2, 2, nx, nz), F32),
            pltpu.VMEM((2, 2, nx, nz), F32),
            pltpu.SMEM(arrays[-1].shape, jnp.int32),
            dma((4,)),
            dma((8,)),
            dma((2, 4)),
            dma((2, 5)),
            dma((4,)),
        ],
        compiler_params=pltpu.CompilerParams(
            collective_id=0, has_side_effects=True, vmem_limit_bytes=40 * 2**20
        ),
    )(*flat)
    outs = pl.pallas_call(
        functools.partial(finish, (nx, ny, nz)),
        out_shape=(block, block, block),
        in_specs=[vmem] * 6,
        out_specs=[hbm] * 3,
        scratch_shapes=[
            pltpu.VMEM((cells + 2 * ny, nz), F32),
            pltpu.VMEM((cells + 2 * ny, nz), F32),
            pltpu.VMEM((cells, nz), F32),
            pltpu.VMEM((cells, nz), F32),
            dma((2,)),
        ],
        compiler_params=pltpu.CompilerParams(vmem_limit_bytes=16 * 2**20),
    )(*middle)
    return tuple(o.reshape(nx, ny, nz) for o in outs)


def solution(mesh):
    cut = P("gx", "gy", None)
    names = ("gx", "gy")
    counts = (mesh.shape["gx"], mesh.shape["gy"])
    return jax.shard_map(
        functools.partial(body, counts, names),
        mesh=mesh,
        in_specs=(cut,) * 7 + (P(("gx", "gy")),),
        out_specs=(cut, cut, cut),
        check_vma=False,
    )
```

```python
import functools

import jax
import jax.numpy as jnp
from jax import lax
from jax.experimental import pallas as pl
from jax.experimental.pallas import tpu as pltpu
from jax.sharding import PartitionSpec as P

TILE = 32
SWEEPS = 4
DAMAGE_SWEEPS = 3
CHUNKS = 4
ONE, TWO, PART, INV = range(4)
OWN, DEN, Y_TWO, Y_PART = range(4)
SENDS = 4

capacity = (0.5, 0.5)
couple = (0.3, 0.3)
residual_open = 0.05
harmonic_floor = 0.001
crack_length = 2.0
energy_scale = 2.0
F32 = jnp.float32


def harmonic(left, right):
    return 2.0 * left * right / (left + right + harmonic_floor)


def kernel(
    names,
    sizes,
    p_hbm,
    t_hbm,
    d_hbm,
    k_hbm,
    g_hbm,
    qp_hbm,
    qt_hbm,
    roster_hbm,
    final,
    damage,
    around,
    begin,
    tough,
    listed,
    state0,
    state1,
    state2,
    state3,
    fixed,
    force,
    conduct,
    wx,
    wy,
    wz,
    den,
    inv,
    hwx,
    hwy,
    xface,
    yface,
    ysend0,
    yrecv0,
    xrecv0,
    ysend,
    yrecv,
    xsend,
    xrecv,
    csend,
    crecv,
    known,
    yinv,
    roster,
    in_sem,
    send_sem,
    xr,
    yr,
    cr,
):
    nx, ny, nz, count_x, count_y = sizes
    cells = nx * ny
    state = (state0, state1, state2, state3)
    gx, gy = names
    ix = lax.axis_index(gx)
    iy = lax.axis_index(gy)
    has_x = (ix > 0, ix < count_x - 1)
    has_y = (iy > 0, iy < count_y - 1)
    to_x = ({gx: ix - 1}, {gx: ix + 1})
    to_y = ({gy: iy - 1}, {gy: iy + 1})
    corners = [(sx, sy) for sx in range(2) for sy in range(2)]
    has_c = [has_x[sx] & has_y[sy] for sx, sy in corners]
    to_c = [to_x[sx] | to_y[sy] for sx, sy in corners]
    mesh_type = pl.DeviceIdType.MESH

    barrier = pltpu.get_barrier_semaphore()
    for has, to in ((has_y, to_y), (has_x, to_x)):
        for side in range(2):

            @pl.when(has[side])
            def _():
                pl.semaphore_signal(barrier, inc=1, device_id=to[side], device_id_type=mesh_type)

    load = pltpu.make_async_copy
    first = [
        load(d_hbm, damage.at[pl.ds(ny, cells)], in_sem.at[0]),
        load(k_hbm, fixed.at[0], in_sem.at[0]),
        load(p_hbm, state[0].at[0], in_sem.at[0]),
        load(t_hbm, state[0].at[1], in_sem.at[0]),
    ]
    rates = [
        load(qp_hbm, fixed.at[1], in_sem.at[1]),
        load(qt_hbm, fixed.at[2], in_sem.at[1]),
    ]
    late = [
        load(g_hbm, tough, in_sem.at[2]),
        load(roster_hbm, roster, in_sem.at[3]),
    ]
    for copy in first + rates + late:
        copy.start()

    def arrived(ref, sem):
        pltpu.make_async_copy(ref, ref, sem).wait()

    csend[...] = jnp.zeros(csend.shape, F32)
    for c in range(4):

        @pl.when(jnp.logical_not(has_c[c]))
        def _():
            crecv[c] = jnp.zeros(crecv.shape[1:], F32)

    for side in range(2):

        @pl.when(jnp.logical_not(has_x[side]))
        def _():
            xrecv0[side] = jnp.zeros(xrecv0.shape[1:], F32)
            for step in range(SENDS):
                xrecv[side, step] = jnp.zeros(xrecv.shape[2:], F32)

        @pl.when(jnp.logical_not(has_y[side]))
        def _():
            yrecv0[side] = jnp.zeros(yrecv0.shape[1:], F32)
            for step in range(SENDS):
                yrecv[side, step] = jnp.full(yrecv.shape[2:], float(step == DEN), F32)

    zero_plane = jnp.zeros((ny, nz), F32)
    damage[0:ny] = zero_plane
    damage[(nx + 1) * ny : (nx + 2) * ny] = zero_plane
    for f in range(2):
        wx[f, 0:ny] = zero_plane
        wx[f, nx * ny : (nx + 1) * ny] = zero_plane

    def rows(r, first_plane=0):
        return pl.ds(first_plane * ny + r, nx, stride=ny)

    def plane(i):
        return pl.ds(i * ny, ny)

    edge_row = (rows(0), rows(ny - 1))
    next_row = (rows(1), rows(ny - 2))
    edge_plane = (plane(0), plane(nx - 1))
    next_plane = (plane(1), plane(nx - 2))
    edge_pad = (rows(0, 1), rows(ny - 1, 1))
    edge_plane_pad = (plane(1), plane(nx))

    arrived(wy, in_sem.at[0])

    for side in range(2):
        ysend0[side, 0 * nx : 1 * nx] = damage[edge_pad[side], :]
        ysend0[side, 1 * nx : 2 * nx] = fixed.at[0][edge_row[side], :]
        ysend0[side, 2 * nx : 3 * nx] = state[0].at[0][edge_row[side], :]
        ysend0[side, 3 * nx : 4 * nx] = state[0].at[1][edge_row[side], :]

    def remote(source, target, send, recv, to):
        return pltpu.make_async_remote_copy(
            src_ref=source,
            dst_ref=target,
            send_sem=send,
            recv_sem=recv,
            device_id=to,
            device_id_type=mesh_type,
        )

    place = {ONE: 1, TWO: 2, PART: 3, INV: 3}

    def send_y(step, count, side):
        @pl.when(has_y[side])
        def _():
            remote(
                ysend.at[side, pl.ds(step, count)],
                yrecv.at[1 - side, pl.ds(step, count)],
                send_sem.at[2 + side],
                yr.at[1 - side, {OWN: 1, Y_TWO: 2, Y_PART: 3}[step]],
                to_y[side],
            ).start()

    def send_x(step, side, source):
        @pl.when(has_x[side])
        def _():
            remote(
                source,
                xrecv.at[1 - side, step],
                send_sem.at[side],
                xr.at[1 - side, place[step]],
                to_x[side],
            ).start()

    def wait_y(side, ref, n):
        @pl.when(has_y[side])
        def _():
            arrived(ref, yr.at[side, n])

    def wait_x(side, ref, n):
        @pl.when(has_x[side])
        def _():
            arrived(ref, xr.at[side, n])

    peers = sum(jnp.where(has, 1, 0).astype(jnp.int32) for has in has_x + has_y)
    pl.semaphore_wait(barrier, peers)

    for side in range(2):

        @pl.when(has_y[side])
        def _():
            remote(
                ysend0.at[side],
                yrecv0.at[1 - side],
                send_sem.at[2 + side],
                yr.at[1 - side, 0],
                to_y[side],
            ).start()

    for side in range(2):
        sources = (
            damage.at[edge_plane_pad[side]],
            fixed.at[0, edge_plane[side]],
            state[0].at[0, edge_plane[side]],
            state[0].at[1, edge_plane[side]],
        )

        @pl.when(has_x[side])
        def _():
            for n, source in enumerate(sources):
                remote(
                    source,
                    xrecv0.at[1 - side, pl.ds(n * ny, ny)],
                    send_sem.at[side],
                    xr.at[1 - side, 0],
                    to_x[side],
                ).start()

    row = lax.broadcasted_iota(jnp.int32, (ny, nz), 0)
    lane = lax.broadcasted_iota(jnp.int32, (ny, nz), 1)

    def at(i):
        return pl.ds(pl.multiple_of(i * ny, ny), ny)

    def open_of(d):
        return (1.0 - d) * (1.0 - d) + residual_open

    arrived(fixed.at[pl.ds(1, 2)], in_sem.at[1])

    @pl.loop(0, nx, unroll=8)
    def _(i):
        openness = open_of(damage[at(i + 1)])
        conduct[1, at(i)] = openness
        conduct[0, at(i)] = fixed[0, at(i)] * openness
        for f in range(2):
            force[f, at(i)] = fixed[1 + f, at(i)] + capacity[f] * state[0][f, at(i)]

    @pl.loop(0, nx, unroll=8)
    def _(i):
        follow = jnp.minimum(i + 1, nx - 1)
        inside = jnp.where(i < nx - 1, 1.0, 0.0).astype(F32)
        for f in range(2):
            own = conduct[f, at(i)]
            ahead = harmonic(own, conduct[f, at(follow)]) * inside
            wx[f, at(i + 1)] = ahead
            y_hi = jnp.where(row < ny - 1, harmonic(own, pltpu.roll(own, ny - 1, 0)), 0.0)
            y_lo = pltpu.roll(y_hi, 1, 0)
            z_hi = jnp.where(lane < nz - 1, harmonic(own, pltpu.roll(own, nz - 1, 1)), 0.0)
            z_lo = pltpu.roll(z_hi, 1, 1)
            wy[f, 0, at(i)] = y_lo
            wy[f, 1, at(i)] = y_hi
            wz[f, 0, at(i)] = z_lo
            wz[f, 1, at(i)] = z_hi
            total = capacity[f] + ahead + wx[f, at(i)] + y_lo + y_hi + z_lo + z_hi
            den[f, at(i)] = total
            inv[f, at(i)] = 1.0 / total

    levels = state + (final,)

    def sweep(step, start=0, stop=nx):
        @pl.loop(start, stop, unroll=16)
        def _(i):
            before = jnp.maximum(i - 1, 0)
            follow = jnp.minimum(i + 1, nx - 1)
            center = [state[step][f, at(i)] for f in range(2)]
            for f in range(2):
                c = center[f]
                acc = force[f, at(i)] + couple[f] * center[1 - f]
                acc = acc + wx[f, at(i)] * state[step][f, at(before)]
                acc = acc + wx[f, at(i + 1)] * state[step][f, at(follow)]
                acc = acc + wy[f, 0, at(i)] * pltpu.roll(c, 1, 0)
                acc = acc + wy[f, 1, at(i)] * pltpu.roll(c, ny - 1, 0)
                acc = acc + wz[f, 0, at(i)] * pltpu.roll(c, 1, 1)
                acc = acc + wz[f, 1, at(i)] * pltpu.roll(c, nz - 1, 1)
                levels[step + 1][f, at(i)] = acc * inv[f, at(i)]

    for side in range(2):
        wait_x(side, xrecv0.at[side], 0)

    for side in range(2):
        there = jnp.where(has_x[side], 1.0, 0.0).astype(F32)
        openness = open_of(xrecv0[side, 0:ny]) * there
        halo_conduct = (xrecv0[side, ny : 2 * ny] * openness, openness)
        for f in range(2):
            hwx[f, side] = harmonic(conduct[f, edge_plane[side]], halo_conduct[f])

    def ends(count, low, high):
        spot = lax.broadcasted_iota(jnp.int32, (count, nz), 0)
        return jnp.where(spot == 0, low, jnp.where(spot == count - 1, high, 0.0))

    sweep(0)

    for side in range(2):
        cut = edge_row[side]
        r = side * (ny - 1)
        own = [ysend0[side, (2 + f) * nx : (3 + f) * nx] for f in range(2)]
        for f in range(2):
            both = slice(f * nx, (f + 1) * nx)
            weight = [hwx[f, sx, r : r + 1] for sx in range(2)]
            flow = [
                weight[sx] * xrecv0[sx, (2 + f) * ny + r : (2 + f) * ny + r + 1] for sx in range(2)
            ]
            ysend[side, DEN, both] = den.at[f][cut, :] + ends(nx, *weight)
            ysend[side, OWN, both] = (
                force.at[f][cut, :]
                + couple[f] * own[1 - f]
                + wx.at[f][rows(r), :] * pltpu.roll(own[f], 1, 0)
                + wx.at[f][rows(r, 1), :] * pltpu.roll(own[f], nx - 1, 0)
                + wy.at[f, 1 - side][cut, :] * state[0].at[f][next_row[side], :]
                + wz.at[f, 0][cut, :] * pltpu.roll(own[f], 1, 1)
                + wz.at[f, 1][cut, :] * pltpu.roll(own[f], nz - 1, 1)
                + ends(nx, *flow)
            )
        send_y(OWN, 2, side)

    for side in range(2):
        cut = edge_plane[side]
        for f in range(2):
            w = hwx[f, side]
            old = den[f, cut]
            total = old + w
            inverse = 1.0 / total
            den[f, cut] = total
            inv[f, cut] = inverse
            value = xrecv0[side, (2 + f) * ny : (3 + f) * ny]
            state[1][f, cut] = (state[1][f, cut] * old + w * value) * inverse

    for side in range(2):
        wait_y(side, yrecv0.at[side], 0)

    for side in range(2):
        there = jnp.where(has_y[side], 1.0, 0.0).astype(F32)
        openness = open_of(yrecv0[side, 0:nx]) * there
        halo_conduct = (yrecv0[side, nx : 2 * nx] * openness, openness)
        cut = edge_row[side]
        for f in range(2):
            w = harmonic(conduct.at[f][cut, :], halo_conduct[f])
            hwy[f, side] = w
            old = den.at[f][cut, :]
            inverse = 1.0 / (old + w)
            inv.at[f][cut, :] = inverse
            known[side, f] = w * ysend0[side, (2 + f) * nx : (3 + f) * nx]
            value = yrecv0[side, (2 + f) * nx : (3 + f) * nx]
            state[1].at[f][cut, :] = (state[1].at[f][cut, :] * old + w * value) * inverse
    for side in range(2):
        send_x(ONE, side, state[1].at[:, edge_plane[side]])

    sweep(1)

    for side in range(2):
        send_x(INV, side, inv.at[:, edge_plane[side]])

    for side in range(2):
        for f in range(2):
            cut = edge_plane[side]
            scale = inv[f, cut]
            inner = wx[f, plane(1) if side == 0 else plane(nx - 1)]
            parts = (
                force[f, cut],
                couple[f],
                wy[f, 0, cut],
                wy[f, 1, cut],
                inner,
                wz[f, 0, cut],
                wz[f, 1, cut],
                hwx[f, side],
            )
            for n, part in enumerate(parts):
                xface[side, f, n] = part * scale
            xface[side, f, 8] = inner * inv[f, next_plane[side]]

            cut = edge_row[side]
            scale = inv.at[f][cut, :]
            inner = wy.at[f, 1 - side][cut, :]
            parts = (
                force.at[f][cut, :],
                couple[f],
                wx.at[f][rows(side * (ny - 1)), :],
                wx.at[f][rows(side * (ny - 1), 1), :],
                inner,
                wz.at[f, 0][cut, :],
                wz.at[f, 1][cut, :],
                hwy[f, side],
            )
            for n, part in enumerate(parts):
                yface[side, f, n] = part * scale
            yface[side, f, 8] = inner * inv.at[f][next_row[side], :]

    def along(face, n, own):
        return (
            face[2] * pltpu.roll(own, 1, 0)
            + face[3] * pltpu.roll(own, n - 1, 0)
            + face[5] * pltpu.roll(own, 1, 1)
            + face[6] * pltpu.roll(own, nz - 1, 1)
        )

    for side in range(2):
        wait_x(side, xrecv.at[side, ONE], 1)
    for side in range(2):
        cut = edge_plane[side]
        for f in range(2):
            value = xrecv[side, ONE, f]
            state[2][f, cut] = state[2][f, cut] + xface[side, f, 7] * value
    for side in range(2):
        wait_y(side, yrecv.at[side, pl.ds(OWN, 2)], 1)
        for f in range(2):
            cut = edge_row[side]
            both = slice(f * nx, (f + 1) * nx)
            inverse = 1.0 / (yrecv[side, DEN, both] + hwy[f, side])
            yinv[side, f] = inverse
            value = (yrecv[side, OWN, both] + known[side, f]) * inverse
            fresh = state[2].at[f][cut, :] + yface[side, f, 7] * value
            state[2].at[f][cut, :] = fresh
            ysend[side, Y_TWO, both] = fresh
        send_y(Y_TWO, 1, side)
        own = [ysend[side, Y_TWO, f * nx : (f + 1) * nx] for f in range(2)]
        for f in range(2):
            face = yface.at[side, f]
            inner = state[2].at[f][next_row[side], :]
            value = face[0] + face[1] * own[1 - f] + face[4] * inner + along(face, nx, own[f])
            ysend[side, Y_PART, f * nx : (f + 1) * nx] = value
        send_y(Y_PART, 1, side)
    for side in range(2):
        send_x(TWO, side, state[2].at[:, edge_plane[side]])

    for c, (sx, sy) in enumerate(corners):
        xe = sx * (nx - 1)
        ye = sy * (ny - 1)
        for f in range(2):
            value = state[2][f, pl.ds(xe * ny + ye, 1), :]
            csend[c, f : f + 1] = hwx[f, sx, ye : ye + 1] * value
            csend[c, 2 + f : 3 + f] = hwy[f, sy, xe : xe + 1] * value

        @pl.when(has_c[c])
        def _():
            remote(csend.at[c], crecv.at[3 - c], send_sem.at[4 + c], cr.at[3 - c], to_c[c]).start()

    for side in range(2):
        own = [state[2][f, edge_plane[side]] for f in range(2)]
        for f in range(2):
            face = xface.at[side, f]
            inner = state[2][f, next_plane[side]]
            value = face[0] + face[1] * own[1 - f] + face[4] * inner + along(face, ny, own[f])
            xsend[side, f] = value
        send_x(PART, side, xsend.at[side])

    sweep(2)
    sweep(3)

    at_low = lane % TILE == 0
    at_high = lane % TILE == TILE - 1

    @pl.loop(0, nx, unroll=8)
    def _(i):
        d = damage[at(i + 1)]
        low = jnp.where(at_low & (lane > 0), pltpu.roll(d, 1, 1), 0.0)
        high = jnp.where(at_high & (lane < nz - 1), pltpu.roll(d, nz - 1, 1), 0.0)
        around[at(i)] = low + high

    for side in range(2):
        around[edge_plane[side], :] = around[edge_plane[side], :] + xrecv0[side, 0:ny]
    for side in range(2):
        around[edge_row[side], :] = around[edge_row[side], :] + yrecv0[side, 0:nx]
    arrived(tough, in_sem.at[2])
    arrived(roster, in_sem.at[3])
    tile_of = lane // TILE
    chosen = tile_of == roster[0]
    for n in range(1, roster.shape[0]):
        chosen = chosen | (tile_of == roster[n])
    listed[...] = jnp.where(chosen, 1.0, 0.0)

    @pl.loop(0, nx, unroll=8)
    def _(i):
        d = damage[at(i + 1)]
        near = around[at(i)] + damage[at(i)] + damage[at(i + 2)]
        near = near + jnp.where(row == 0, 0.0, pltpu.roll(d, 1, 0))
        near = near + jnp.where(row == ny - 1, 0.0, pltpu.roll(d, ny - 1, 0))
        near = near + jnp.where(at_low, 0.0, pltpu.roll(d, 1, 1))
        near = near + jnp.where(at_high, 0.0, pltpu.roll(d, nz - 1, 1))
        begin[at(i)] = near

    for side in range(2):
        wait_x(side, xrecv.at[side, TWO], 2)
    for side in range(2):
        cut = edge_plane[side]
        cut_in = next_plane[side]
        change = [
            xface[side, f, 7] * xrecv[side, TWO, f] for f in range(2)
        ]
        for f in range(2):
            face = xface.at[side, f]
            add = face[1] * change[1 - f] + along(face, ny, change[f])
            final[f, cut] = final[f, cut] + add
            final[f, cut_in] = final[f, cut_in] + face[8] * change[f]

    for side in range(2):
        wait_y(side, yrecv.at[side, Y_TWO], 2)
        cut = edge_row[side]
        cut_in = next_row[side]
        change = [
            yface[side, f, 7] * yrecv[side, Y_TWO, f * nx : (f + 1) * nx] for f in range(2)
        ]
        for f in range(2):
            face = yface.at[side, f]
            add = face[1] * change[1 - f] + along(face, nx, change[f])
            final.at[f][cut, :] = final.at[f][cut, :] + add
            final.at[f][cut_in, :] = final.at[f][cut_in, :] + face[8] * change[f]

    for side in range(2):
        wait_x(side, xrecv.at[side, pl.ds(PART, 2)], 3)
    for c in range(4):

        @pl.when(has_c[c])
        def _():
            arrived(crecv.at[c], cr.at[c])

    for side in range(2):
        cut = edge_plane[side]
        for f in range(2):
            more = ends(
                ny, crecv[2 * side, 2 + f : 3 + f], crecv[2 * side + 1, 2 + f : 3 + f]
            )
            beyond = xrecv[side, PART, f] + xrecv[side, INV, f] * (
                hwx[f, side] * state[2][f, cut] + more
            )
            final[f, cut] = final[f, cut] + xface[side, f, 7] * beyond

    for side in range(2):
        wait_y(side, yrecv.at[side, Y_PART], 3)
        cut = edge_row[side]
        for f in range(2):
            both = slice(f * nx, (f + 1) * nx)
            more = ends(nx, crecv[side, f : f + 1], crecv[2 + side, f : f + 1])
            more = more + hwy[f, side] * ysend[side, Y_TWO, both]
            beyond = yrecv[side, Y_PART, both] + yinv[side, f] * more
            final.at[f][cut, :] = final.at[f][cut, :] + yface[side, f, 7] * beyond

    for c in range(4):

        @pl.when(has_c[c])
        def _():
            arrived(csend.at[c], send_sem.at[4 + c])

    for side in range(2):

        @pl.when(has_y[side])
        def _():
            arrived(fixed.at[0, pl.ds(0, (4 + 2 * SENDS) * nx)], send_sem.at[2 + side])

        @pl.when(has_x[side])
        def _():
            arrived(fixed.at[0, pl.ds(0, (4 + 2 * SENDS) * ny)], send_sem.at[side])


def finish(
    sizes,
    final,
    damage,
    around,
    begin,
    tough,
    listed,
    p_out,
    t_out,
    d_out,
    work0,
    work1,
    da,
    db,
    out_sem,
):
    nx, ny, nz = sizes
    cells = nx * ny
    row = lax.broadcasted_iota(jnp.int32, (ny, nz), 0)
    lane = lax.broadcasted_iota(jnp.int32, (ny, nz), 1)

    def at(i):
        return pl.ds(pl.multiple_of(i * ny, ny), ny)

    outs = [
        pltpu.make_async_copy(final.at[0], p_out, out_sem.at[0]),
        pltpu.make_async_copy(final.at[1], t_out, out_sem.at[0]),
    ]
    for out in outs:
        out.start()

    zero_plane = jnp.zeros((ny, nz), F32)
    for work in (work0, work1):
        work[0:ny] = zero_plane
        work[(nx + 1) * ny : (nx + 2) * ny] = zero_plane

    y_first = row == 0
    y_last = row == ny - 1
    z_first = lane % TILE == 0
    z_last = lane % TILE == TILE - 1
    inside = listed[...] > 0.0

    piece = cells // CHUNKS
    last = [
        pltpu.make_async_copy(
            work0.at[pl.ds(ny + chunk * piece, piece)],
            d_out.at[pl.ds(chunk * piece, piece)],
            out_sem.at[1],
        )
        for chunk in range(CHUNKS)
    ]
    for step in range(DAMAGE_SWEEPS):
        source = (damage, work0, work1)[step % 3]
        target = (work0, work1, work0)[step % 3]

        def relax(i):
            d = source[at(i + 1)]
            if step == 0:
                near = begin[at(i)]
            else:
                near = around[at(i)] + source[at(i)] + source[at(i + 2)]
                near = near + jnp.where(y_first, 0.0, pltpu.roll(d, 1, 0))
                near = near + jnp.where(y_last, 0.0, pltpu.roll(d, ny - 1, 0))
                near = near + jnp.where(z_first, 0.0, pltpu.roll(d, 1, 1))
                near = near + jnp.where(z_last, 0.0, pltpu.roll(d, nz - 1, 1))
            if step == 0:
                load = final[0, at(i)]
                hard = tough[at(i)]
                drive = 2.0 * energy_scale * load * load
                spread = hard * crack_length
                inverse = 1.0 / (hard / crack_length + drive + 6.0 * spread)
                a = drive * inverse
                b = spread * inverse
                da[at(i)] = a
                db[at(i)] = b
            else:
                a = da[at(i)]
                b = db[at(i)]
            fresh = a + b * near
            if step == DAMAGE_SWEEPS - 1:
                fresh = jnp.where(inside, fresh, damage[at(i + 1)])
            target[at(i + 1)] = fresh

        if step < DAMAGE_SWEEPS - 1:
            pl.loop(0, nx, unroll=nx)(relax)
        else:
            for chunk in range(CHUNKS):
                pl.loop(chunk * nx // CHUNKS, (chunk + 1) * nx // CHUNKS, unroll=nx // CHUNKS)(relax)
                last[chunk].start()

    pltpu.make_async_copy(final, final, out_sem.at[0]).wait()
    whole = work0.at[pl.ds(ny, cells)]
    pltpu.make_async_copy(whole, whole, out_sem.at[1]).wait()


def body(counts, names, *arrays):
    nx, ny, nz = arrays[0].shape
    cells = nx * ny
    flat = [a.reshape(cells, nz) for a in arrays[:-1]] + [arrays[-1]]
    flat = [pltpu.with_memory_space_constraint(a, pltpu.HBM) for a in flat]
    block = jax.ShapeDtypeStruct((cells, nz), F32)
    dma = pltpu.SemaphoreType.DMA
    vmem = pl.BlockSpec(memory_space=pltpu.VMEM)
    hbm = pl.BlockSpec(memory_space=pl.ANY)
    middle = pl.pallas_call(
        functools.partial(kernel, names, (nx, ny, nz) + counts),
        out_shape=(
            jax.ShapeDtypeStruct((2, cells, nz), F32),
            jax.ShapeDtypeStruct((cells + 2 * ny, nz), F32),
            block,
            block,
            block,
            jax.ShapeDtypeStruct((ny, nz), F32),
        ),
        in_specs=[hbm] * 8,
        out_specs=[vmem] * 6,
        scratch_shapes=[
            pltpu.VMEM((2, cells, nz), F32),
            pltpu.VMEM((2, cells, nz), F32),
            pltpu.VMEM((2, cells, nz), F32),
            pltpu.VMEM((2, cells, nz), F32),
            pltpu.VMEM((3, cells, nz), F32),
            pltpu.VMEM((2, cells, nz), F32),
            pltpu.VMEM((2, cells, nz), F32),
            pltpu.VMEM((2, cells + ny, nz), F32),
            pltpu.VMEM((2, 2, cells, nz), F32),
            pltpu.VMEM((2, 2, cells, nz), F32),
            pltpu.VMEM((2, cells, nz), F32),
            pltpu.VMEM((2, cells, nz), F32),
            pltpu.VMEM((2, 2, ny, nz), F32),
            pltpu.VMEM((2, 2, nx, nz), F32),
            pltpu.VMEM((2, 2, 9, ny, nz), F32),
            pltpu.VMEM((2, 2, 9, nx, nz), F32),
            pltpu.VMEM((2, 4 * nx, nz), F32),
            pltpu.VMEM((2, 4 * nx, nz), F32),
            pltpu.VMEM((2, 4 * ny, nz), F32),
            pltpu.VMEM((2, SENDS, 2 * nx, nz), F32),
            pltpu.VMEM((2, SENDS, 2 * nx, nz), F32),
            pltpu.VMEM((2, 2, ny, nz), F32),
            pltpu.VMEM((2, SENDS, 2, ny, nz), F32),
            pltpu.VMEM((4, 8, nz), F32),
            pltpu.VMEM((4, 8, nz), F32),
            pltpu.VMEM((2, 2, nx, nz), F32),
            pltpu.VMEM((2, 2, nx, nz), F32),
            pltpu.SMEM(arrays[-1].shape, jnp.int32),
            dma((4,)),
            dma((8,)),
            dma((2, 4)),
            dma((2, 4)),
            dma((4,)),
        ],
        compiler_params=pltpu.CompilerParams(
            collective_id=0, has_side_effects=True, vmem_limit_bytes=40 * 2**20
        ),
    )(*flat)
    outs = pl.pallas_call(
        functools.partial(finish, (nx, ny, nz)),
        out_shape=(block, block, block),
        in_specs=[vmem] * 6,
        out_specs=[hbm] * 3,
        scratch_shapes=[
            pltpu.VMEM((cells + 2 * ny, nz), F32),
            pltpu.VMEM((cells + 2 * ny, nz), F32),
            pltpu.VMEM((cells, nz), F32),
            pltpu.VMEM((cells, nz), F32),
            dma((2,)),
        ],
        compiler_params=pltpu.CompilerParams(vmem_limit_bytes=16 * 2**20),
    )(*middle)
    return tuple(o.reshape(nx, ny, nz) for o in outs)


def solution(mesh):
    cut = P("gx", "gy", None)
    names = ("gx", "gy")
    counts = (mesh.shape["gx"], mesh.shape["gy"])
    return jax.shard_map(
        functools.partial(body, counts, names),
        mesh=mesh,
        in_specs=(cut,) * 7 + (P(("gx", "gy")),),
        out_specs=(cut, cut, cut),
        check_vma=False,
    )
```
